128 devices in a mesh: lat: 16 (over z, x_lo, core), vec: 8 (over x_hi, y).
Axes of the slice: x: 4 (x_hi: 2, x_lo: 2; x = x_hi * 2 + x_lo), y: 4, z: 4, core: 2. Of those that a mesh axis runs over, the one named last changes fastest.
Arguments:
- vectors: bfloat16 [4, 128, 256, 1024], P(None, 'vec', 'lat'), may hold values from -6 to 6
- classical_spins: float32 [3, 256, 1024], P(None, 'lat'), may hold values from -1 to 1, as said below
- coefficients: float32 [5], replicated, may hold values from 0.4 to 1.6
Outputs:
- rotated_spins: float32 [3, 256, 1024], P(None, 'lat')
- local_fields: float32 [3, 256, 1024], P(None, 'lat')
The draws below stay inside these ranges and needn't reach their ends.
Inputs may be any that keep to these rules, and one draw needn't show every extreme that they name: `classical_spins`: each site's spin has unit length.
All inputs are finite; a program needn't handle non-finite values.
Results may differ from the reference program's by a relative error of at most 0.0003.
Values sent between devices are 32-bit elements; how exact they have to be, the bound alone decides.
A program may use at most 64 MiB of HBM per device.

```python
import jax
import jax.numpy as jnp
from jax import lax

NY = 1024
R_DEV = 16
STEPS = 4
NX = 256
VECTORS = 128
N_VEC = 8


def draw_classical_spins(key, part):
    raw = jax.random.normal(key, (3, NX, NY), jnp.float32)
    length = jnp.sqrt(jnp.sum(raw * raw, axis=0, keepdims=True))
    return raw / jnp.maximum(length, 0.001)


def shard_levels(rng, extent, shards, smallest, largest):
    factor_of = 1.0
    for axis_at, shards_of in shards:
        heights = jax.random.uniform(jax.random.fold_in(jax.random.fold_in(rng, 6), axis_at), (shards_of,), jnp.float32, smallest / len(shards), largest / len(shards))
        factor_of = factor_of * jnp.repeat(jnp.exp(heights), extent[axis_at] // shards_of).reshape((-1,) + (1,) * (len(extent) - 1 - axis_at))
    return factor_of


def gaussian(stream_key, extent, deviation, reach, pieces=(), dtype=jnp.bfloat16):
    level = shard_levels(stream_key, extent, pieces, -0.22, 0.18) if pieces else 1.0
    values = jax.random.normal(stream_key, extent, jnp.float32) * deviation * level
    return jnp.minimum(jnp.maximum(values, -reach), reach).astype(dtype)


def setup_inputs(seed: int = 0) -> dict:
    keys = jax.random.split(jax.random.key(seed), 4)
    return {
        "vectors": gaussian(keys[0], (4, VECTORS, NX, NY), 0.7071, 6.0, ((1, 8), (2, 16))),
        "classical_spins": draw_classical_spins(jax.random.fold_in(keys[3], 71), 0),
        "coefficients": jnp.clip(jax.random.uniform(keys[2], (STEPS + 1,), jnp.float32, 0.4, 1.6), 0.4, 1.6),
    }


coupling = 2.0
hopping = 1.0
inverse_bound = 1.0 / 6.5
time_step = 1.0

def exchange_term(states, spins_here):
    spin_x = spins_here[0][None]
    spin_y = spins_here[1][None]
    spin_z = spins_here[2][None]
    up_real, up_imag, down_real, down_imag = (states[0], states[1], states[2], states[3])
    return jnp.stack([spin_z * up_real + spin_x * down_real + spin_y * down_imag, spin_z * up_imag + spin_x * down_imag - spin_y * down_real, spin_x * up_real - spin_y * up_imag - spin_z * down_real, spin_x * up_imag + spin_y * up_real - spin_z * down_imag])

def spin_density(probes, weighted):
    along_x = lax.optimization_barrier(jnp.sum(probes[0] * weighted[2] + probes[1] * weighted[3] + probes[2] * weighted[0] + probes[3] * weighted[1], axis=0))
    along_y = lax.optimization_barrier(jnp.sum(probes[0] * weighted[3] - probes[1] * weighted[2] - probes[2] * weighted[1] + probes[3] * weighted[0], axis=0))
    along_z = lax.optimization_barrier(jnp.sum(probes[0] * weighted[0] + probes[1] * weighted[1] - probes[2] * weighted[2] - probes[3] * weighted[3], axis=0))
    return jnp.stack([along_x, along_y, along_z])

def rotate_spins(spins_now, fields):
    magnitude = jnp.sqrt(lax.optimization_barrier(jnp.sum(fields * fields, axis=0)))
    rotation_angle = time_step * magnitude
    cosine = jnp.cos(rotation_angle)
    sine_ratio = jnp.sinc(rotation_angle / jnp.pi)
    half_ratio = 0.5 * jnp.sinc(rotation_angle / (2.0 * jnp.pi)) ** 2
    torque = jnp.cross(fields, spins_now, axis=0)
    projection = lax.optimization_barrier(jnp.sum(fields * spins_now, axis=0))
    return cosine * spins_now + time_step * sine_ratio * torque + time_step * time_step * half_ratio * projection * fields

def reference(vectors, classical_spins, coefficients):

    def hamiltonian(states):
        neighbours = jnp.roll(states, 1, 2) + jnp.roll(states, -1, 2) + jnp.roll(states, 1, 3) + jnp.roll(states, -1, 3)
        return inverse_bound * (coupling * exchange_term(states, classical_spins) - hopping * neighbours)

    def one_block(block_index, summed):
        offset = block_index * R_DEV
        probes = lax.dynamic_slice_in_dim(vectors, offset, R_DEV, 1).astype(jnp.float32)
        previous = probes
        current = probes
        moments = coefficients[0] * probes
        for degree in range(STEPS):
            if degree == 0:
                following = hamiltonian(current)
            else:
                following = 2.0 * hamiltonian(current) - previous
            moments = moments + coefficients[degree + 1] * following
            previous, current = (current, following)
        return summed + spin_density(probes, moments)
    summed = lax.fori_loop(0, N_VEC, one_block, jnp.zeros((3, NX, NY), jnp.float32))
    fields = summed * (coupling / (R_DEV * N_VEC))
    return (rotate_spins(classical_spins, fields), fields)
```

```python
import functools

import jax
import jax.numpy as jnp
from jax import lax
from jax.experimental import pallas as pl
from jax.experimental.pallas import tpu as pltpu
from jax.sharding import PartitionSpec as P

MESH = pl.DeviceIdType.MESH
LAT, VEC = 16, 8
ROWS, COLS, VECS = 16, 1024, 16
BLOCKS = COLS // 128
PAD = 4
coupling = 2.0
inverse_bound = 1.0 / 6.5


def spin_on(state, spin):
    x, y, z = spin
    p0, p1, p2, p3 = state
    return (
        (z * p0 + x * p2) + y * p3,
        (z * p1 + x * p3) - y * p2,
        (x * p0 - y * p1) - z * p2,
        (x * p1 + y * p0) - z * p3,
    )


def density(r, w):
    return (
        (r[0] * w[2] + r[1] * w[3]) + (r[2] * w[0] + r[3] * w[1]),
        (r[0] * w[3] - r[1] * w[2]) - (r[2] * w[1] - r[3] * w[0]),
        (r[0] * w[0] + r[1] * w[1]) - (r[2] * w[2] + r[3] * w[3]),
    )


def lanes(j):
    j = j % BLOCKS
    return slice(j * 128, (j + 1) * 128)


def field_kernel(
    coef, x_hbm, s_vmem, out,
    xv, R, W3, W2, W1, SB, SHs, SHr, D, E, PBs, PBr, FP, RB, SUM,
    xsem, hs, hr, ss, sr, ps, pr, rs_s, rs_r, ag_s, ag_r,
):
    lat, vec = lax.axis_index("lat"), lax.axis_index("vec")
    prev, nxt = lax.rem(lat + LAT - 1, LAT), lax.rem(lat + 1, LAT)

    load = pltpu.make_async_copy(x_hbm, xv, xsem)
    load.start()

    barrier = pltpu.get_barrier_semaphore()
    for to in (prev, nxt):
        pl.semaphore_signal(barrier, 1, device_id={"lat": to}, device_id_type=MESH)
    for d in range(1, VEC):
        pl.semaphore_signal(
            barrier, 1, device_id={"vec": lax.rem(vec + d, VEC)}, device_id_type=MESH
        )

    c0, c1, c2, c3, c4 = (coef[k] for k in range(5))
    h = inverse_bound
    a0 = c0 - c2 + c4
    a1 = (3.0 * c3 - c1) * h
    a2 = (2.0 * c2 - 8.0 * c4) * (h * h)
    a3 = c3 * (-4.0 * h * h * h)
    a4 = c4 * (8.0 * h * h * h * h)

    zero = jnp.zeros((8, COLS), jnp.float32)
    for row in range(ROWS):
        for c in range(3):
            SB[PAD + row, c] = jnp.broadcast_to(2.0 * s_vmem[c, row : row + 1, :], (8, COLS))
    for c in range(3):
        for row in (1, 22):
            SB[row, c] = zero
        for k in range(2):
            q = 2 * c + k
            SHs[0, q : q + 1, :] = s_vmem[c, k : k + 1, :]
            SHs[1, q : q + 1, :] = s_vmem[c, 14 + k : 15 + k, :]
    for s in range(2):
        SHs[s, 6:8, :] = jnp.zeros((2, COLS), jnp.float32)
    for g in range(2):
        for row in (0, 1, 22, 23):
            for c in range(4):
                R[g, row, c] = zero
        for s in range(2):
            for j in range(BLOCKS):
                E[s, g, j, 48:64, :] = jnp.zeros((16, 128), jnp.float32)

    m = lax.broadcasted_iota(jnp.int32, (256, 256), 0)
    k = lax.broadcasted_iota(jnp.int32, (256, 256), 1)
    swap = jnp.where((k % 16 == m // 16) & (k // 16 == m % 16), 1.0, 0.0).astype(jnp.bfloat16)
    load.wait()

    @pl.loop(0, 4)
    def _(c):
        for q in range(4):
            cols = slice(q * 256, (q + 1) * 256)
            got = jnp.dot(
                swap, xv[c, :, :, cols].reshape(256, 256), preferred_element_type=jnp.float32
            )
            for row in range(ROWS):
                for g in range(2):
                    R[g, PAD + row, c, :, cols] = got[row * 16 + g * 8 : row * 16 + g * 8 + 8]

    pl.semaphore_wait(barrier, 2 + VEC - 1)

    def spin_copy(s):
        return pltpu.make_async_remote_copy(
            SHs.at[s], SHr.at[1 - s], ss.at[s], sr.at[1 - s],
            device_id={"lat": (prev, nxt)[s]}, device_id_type=MESH,
        )

    def halo_copy(s, g):
        src, dst = ((4, 20), (18, 2))[s]
        return pltpu.make_async_remote_copy(
            R.at[g, pl.ds(src, 2)], R.at[g, pl.ds(dst, 2)], hs.at[s, g], hr.at[1 - s, g],
            device_id={"lat": (prev, nxt)[s]}, device_id_type=MESH,
        )

    for s in range(2):
        spin_copy(s).start()
    for g in range(2):
        for s in range(2):
            halo_copy(s, g).start()

    lane = lax.broadcasted_iota(jnp.int32, (8, 128), 1)
    first, last = lane == 0, lane == 127

    def around(ref, at, j):
        here = ref[at + (slice(None), lanes(j))]
        left = jnp.where(last, ref[at + (slice(None), lanes(j - 1))], here)
        right = jnp.where(first, ref[at + (slice(None), lanes(j + 1))], here)
        return pltpu.roll(left, 1, 1) + pltpu.roll(right, 127, 1)

    def hop(src, g, row, j):
        cols = (slice(None), lanes(j))
        spin = [SB[(PAD + row, c) + cols] for c in range(3)]
        state = [src[(g, PAD + row, c) + cols] for c in range(4)]
        onsite = spin_on(state, spin)
        res = []
        for c in range(4):
            n = src[(g, PAD + row - 1, c) + cols] + src[(g, PAD + row + 1, c) + cols]
            res.append((n + around(src, (g, PAD + row, c), j)) - onsite[c])
        return res

    def sweep(g, starts, counts, slot_shift):
        @pl.loop(0, counts[0])
        def _(i):
            row = starts[0] + i
            for j in range(BLOCKS):
                cols = (slice(None), lanes(j))
                got = hop(R, g, row, j)
                for c in range(4):
                    W3[(g, PAD + row, c) + cols] = a4 * got[c] + a3 * R[(g, PAD + row, c) + cols]

        for level, (src, dst, a) in enumerate(((W3, W2, a2), (W2, W1, a1)), 1):
            @pl.loop(0, counts[level])
            def _(i):
                row = starts[level] + i
                for j in range(BLOCKS):
                    cols = (slice(None), lanes(j))
                    got = hop(src, g, row, j)
                    for c in range(4):
                        dst[(g, PAD + row, c) + cols] = got[c] + a * R[(g, PAD + row, c) + cols]

        @pl.loop(0, counts[3])
        def _(i):
            row = starts[3] + i
            at = pl.multiple_of((row + slot_shift) * 8, 8)
            for j in range(BLOCKS):
                cols = (slice(None), lanes(j))
                got = hop(W1, g, row, j)
                r = [R[(g, PAD + row, c) + cols] for c in range(4)]
                w = [got[c] + a0 * r[c] for c in range(4)]
                for c, d in enumerate(density(r, w)):
                    D[g, c, j, pl.ds(at, 8), :] = d

    def fold(ref, at, start):
        parts = []
        for g in range(2):
            for s in range(8):
                parts.append(ref[at(g) + (pl.ds(start + s, 8, stride=8), slice(None))])
        while len(parts) > 1:
            parts = [parts[i] + parts[i + 1] for i in range(0, len(parts), 2)]
        return parts[0]

    def scatter_copy(grp, d):
        to = lax.rem(vec + d, VEC)
        return pltpu.make_async_remote_copy(
            FP.at[grp, to], RB.at[grp, d], rs_s.at[grp, d], rs_r.at[grp, d],
            device_id={"vec": to}, device_id_type=MESH,
        )

    def gather_copy(grp, d):
        to = lax.rem(vec + d, VEC)
        return pltpu.make_async_remote_copy(
            SUM.at[grp], out.at[grp, vec], ag_s.at[grp, d], ag_r.at[grp, d],
            device_id={"vec": to}, device_id_type=MESH,
        )

    def reduce_and_gather(grp):
        for d in range(1, VEC):
            scatter_copy(grp, d).wait_recv()
        for c in range(3):
            total = FP[grp, vec, c]
            for d in range(1, VEC):
                total = total + RB[grp, d, c]
            SUM[grp, c] = total
            out[grp, vec, c] = total
        for d in range(1, VEC):
            gather_copy(grp, d).start()

    @pl.loop(0, 2)
    def _(g):
        sweep(g, (1, 2, 3, 4), (14, 12, 10, 8), -4)

    @pl.loop(0, BLOCKS)
    def _(j):
        for c in range(3):
            FP[0, j, c] = fold(D, lambda g: (g, c, j), 0)
    for d in range(1, VEC):
        scatter_copy(0, d).start()

    for s in range(2):
        spin_copy(s).wait()
    for s in range(2):
        for c in range(3):
            for k in range(2):
                q = 2 * c + k
                SB[(2, 20)[s] + k, c] = jnp.broadcast_to(2.0 * SHr[s, q : q + 1, :], (8, COLS))

    def push(s, g):
        far, near = 2 + 11 * s + PAD, PAD - 1 + 17 * s
        row_far, row_next = PAD - 2 + 19 * s, PAD + 3 + 9 * s
        base = PAD - 1 + 14 * s
        at0 = [pl.multiple_of((2 * c + 1 - s) * 8, 8) for c in range(3)]
        at1 = [pl.multiple_of((2 * c + s) * 8, 8) for c in range(3)]
        for j in range(BLOCKS):
            cols = (slice(None), lanes(j))
            spin = [
                (SB[(base, c) + cols] + SB[(base + 1, c) + cols])
                + (SB[(base + 2, c) + cols] + SB[(base + 3, c) + cols])
                for c in range(3)
            ]
            b2 = [R[(g, far, c) + cols] for c in range(4)]
            onsite = spin_on(b2, spin)
            u, v = [], []
            for c in range(4):
                more = R[(g, row_next, c) + cols] + 4.0 * around(R, (g, far, c), j)
                u.append(a3 * b2[c] + a4 * (more - onsite[c]))
                v.append(a4 * b2[c])
            r0 = [R[(g, near, c) + cols] for c in range(4)]
            r1 = [R[(g, row_far, c) + cols] for c in range(4)]
            for c, d in enumerate(density(r0, u)):
                E[s, g, j, pl.ds(at0[c], 8), :] = d
            for c, d in enumerate(density(r1, v)):
                E[s, g, j, pl.ds(at1[c], 8), :] = d

    def wait_halo(s, g):
        pltpu.make_async_copy(R.at[g, pl.ds(2, 2)], R.at[g, pl.ds(2, 2)], hr.at[s, g]).wait()

    def push_copy(s):
        return pltpu.make_async_remote_copy(
            PBs.at[s], PBr.at[1 - s], ps.at[s], pr.at[1 - s],
            device_id={"lat": lax.rem(lat + LAT - 1 + 2 * s, LAT)}, device_id_type=MESH,
        )

    def wedge(s, g):
        sweep(g, (18 * s - 3, 16 * s - 2, 14 * s - 1, 12 * s), (4, 4, 4, 4), 12 - 16 * s)

    near_side = 1 - lax.rem(lat, 2)
    for s in (near_side, 1 - near_side):
        wait_halo(s, 0)
        push(s, 0)
        wedge(s, 0)
        wait_halo(s, 1)
        push(s, 1)

        @pl.loop(0, BLOCKS)
        def _(j):
            PBs[s, j] = fold(E, lambda g: (s, g, j), 0)

        push_copy(s).start()
        wedge(s, 1)

    reduce_and_gather(0)

    for s in range(2):
        push_copy(s).wait()

    sub = lax.broadcasted_iota(jnp.int32, (8, 128), 0)
    from_next, from_prev = (sub == 2) | (sub == 3), (sub == 4) | (sub == 5)

    @pl.loop(0, BLOCKS)
    def _(j):
        for c in range(3):
            total = fold(D, lambda g: (g, c, j), 64)
            total = total + jnp.where(from_next, pltpu.roll(PBr[1, j], (2 - 2 * c) % 8, 0), 0.0)
            total = total + jnp.where(from_prev, pltpu.roll(PBr[0, j], (4 - 2 * c) % 8, 0), 0.0)
            FP[1, j, c] = total

    for d in range(1, VEC):
        scatter_copy(1, d).start()
    reduce_and_gather(1)

    for s in range(2):
        for g in range(2):
            halo_copy(s, g).wait_send()
    for grp in range(2):
        for d in range(1, VEC):
            scatter_copy(grp, d).wait_send()
            gather_copy(grp, d).wait()


def rotate_kernel(f_ref, s_ref, rot, fields):
    sub = lax.broadcasted_iota(jnp.int32, (8, 128), 0)
    top = sub < 4
    for j in range(BLOCKS):
        cols = lanes(j)
        mid = [pltpu.roll(f_ref[0, j, c], 4, 0) for c in range(3)]
        edge = [pltpu.roll(f_ref[1, j, c], 4, 0) for c in range(3)]
        for half in range(2):
            rows = slice(half * 8, half * 8 + 8)
            a, b = (edge, mid) if half == 0 else (mid, edge)
            B = [jnp.where(top, a[c], b[c]) * (coupling / (VECS * VEC)) for c in range(3)]
            S = [s_ref[c, rows, cols] for c in range(3)]
            square = B[0] * B[0] + B[1] * B[1] + B[2] * B[2]
            size = jnp.sqrt(square)
            half_angle = 0.5 * size
            sin_h, cos_h = jnp.sin(half_angle), jnp.cos(half_angle)
            some = size > 0.0
            safe = jnp.where(some, size, 1.0)
            ratio = jnp.where(some, sin_h / safe, 0.5)
            cosine = 1.0 - 2.0 * (sin_h * sin_h)
            sine_ratio = 2.0 * (ratio * cos_h)
            along = 2.0 * (ratio * ratio) * (B[0] * S[0] + B[1] * S[1] + B[2] * S[2])
            cross = (
                B[1] * S[2] - B[2] * S[1],
                B[2] * S[0] - B[0] * S[2],
                B[0] * S[1] - B[1] * S[0],
            )
            for c in range(3):
                fields[c, rows, cols] = B[c]
                rot[c, rows, cols] = (cosine * S[c] + sine_ratio * cross[c]) + along * B[c]


def shards(vectors, classical_spins, coefficients):
    f32 = jnp.float32
    vmem = pl.BlockSpec(memory_space=pltpu.VMEM)
    dma = pltpu.SemaphoreType.DMA
    parts = pl.pallas_call(
        field_kernel,
        name="fields",
        out_shape=jax.ShapeDtypeStruct((2, BLOCKS, 3, 8, 128), f32),
        in_specs=[
            pl.BlockSpec(memory_space=pltpu.SMEM),
            pl.BlockSpec(memory_space=pl.ANY),
            vmem,
        ],
        out_specs=vmem,
        scratch_shapes=[
            pltpu.VMEM((4, VECS, ROWS, COLS), jnp.bfloat16),
            *[pltpu.VMEM((2, 24, 4, 8, COLS), f32)] * 4,
            pltpu.VMEM((24, 3, 8, COLS), f32),
            pltpu.VMEM((2, 8, COLS), f32),
            pltpu.VMEM((2, 8, COLS), f32),
            pltpu.VMEM((2, 3, BLOCKS, 128, 128), f32),
            pltpu.VMEM((2, 2, BLOCKS, 64, 128), f32),
            pltpu.VMEM((2, BLOCKS, 8, 128), f32),
            pltpu.VMEM((2, BLOCKS, 8, 128), f32),
            pltpu.VMEM((2, BLOCKS, 3, 8, 128), f32),
            pltpu.VMEM((2, VEC, 3, 8, 128), f32),
            pltpu.VMEM((2, 3, 8, 128), f32),
            dma, dma((2, 2)), dma((2, 2)), dma((2,)), dma((2,)), dma((2,)), dma((2,)),
            dma((2, VEC)), dma((2, VEC)), dma((2, VEC)), dma((2, VEC)),
        ],
        compiler_params=pltpu.CompilerParams(
            collective_id=0, has_side_effects=True, vmem_limit_bytes=60 << 20
        ),
    )(coefficients, vectors, classical_spins)
    out = jax.ShapeDtypeStruct((3, ROWS, COLS), f32)
    rotated, fields = pl.pallas_call(
        rotate_kernel,
        name="rotate",
        out_shape=(out, out),
        in_specs=[vmem, vmem],
        out_specs=(vmem, vmem),
    )(parts, classical_spins)
    return rotated, fields


def solution(mesh):
    placed = (P(None, "vec", "lat", None), P(None, "lat", None), P())
    return jax.shard_map(
        shards,
        mesh=mesh,
        in_specs=placed,
        out_specs=(P(None, "lat", None), P(None, "lat", None)),
        check_vma=False,
    )
```

```python
import functools

import jax
import jax.numpy as jnp
from jax import lax
from jax.experimental import pallas as pl
from jax.experimental.pallas import tpu as pltpu
from jax.sharding import PartitionSpec as P

MESH = pl.DeviceIdType.MESH
LAT, VEC, NY = 16, 8, 4
ROWS, COLS, VECS = 16, 1024, 16
BLOCKS = COLS // 128
PAD = 4
STEPS_EACH = 4
coupling = 2.0
inverse_bound = 1.0 / 6.5


def spin_on(state, spin):
    x, y, z = spin
    p0, p1, p2, p3 = state
    return (
        (z * p0 + x * p2) + y * p3,
        (z * p1 + x * p3) - y * p2,
        (x * p0 - y * p1) - z * p2,
        (x * p1 + y * p0) - z * p3,
    )


def density(r, w):
    return (
        (r[0] * w[2] + r[1] * w[3]) + (r[2] * w[0] + r[3] * w[1]),
        (r[0] * w[3] - r[1] * w[2]) - (r[2] * w[1] - r[3] * w[0]),
        (r[0] * w[0] + r[1] * w[1]) - (r[2] * w[2] + r[3] * w[3]),
    )


def bf16_parts(x):
    high = x.astype(jnp.bfloat16)
    rest = x - high.astype(jnp.float32)
    mid = rest.astype(jnp.bfloat16)
    low = (rest - mid.astype(jnp.float32)).astype(jnp.bfloat16)
    return jnp.concatenate([high, mid, low], axis=0)


def permuted(x, by):
    n = x.shape[0]
    got = jnp.dot(bf16_parts(x), by, preferred_element_type=jnp.float32)
    return (got[:n] + got[n : 2 * n]) + got[2 * n :]


def deal(inverse=False):
    here = lax.broadcasted_iota(jnp.int32, (256, 256), int(inverse))
    there = lax.broadcasted_iota(jnp.int32, (256, 256), int(not inverse))
    source = jnp.where(there < 128, 2 * there, 2 * there - 255)
    return jnp.where(here == source, 1.0, 0.0).astype(jnp.bfloat16)


def lanes(j):
    j = j % BLOCKS
    return slice(j * 128, (j + 1) * 128)


def field_kernel(
    coef, x_hbm, s_vmem, out_mid, out_edge,
    xv, R, W3, W2, W1, SB, SHs, SHr, DM, DE, E, PBs, PBr,
    FM, RM, QM, XM, FE, RE, QE, XE, SP, RB,
    xsem, hs, hr, ss, sr, ps, pr, ys_s, ys_r, xs_s, xs_r, yg_s, yg_r, bs_s, bs_r,
):
    lat, vec = lax.axis_index("lat"), lax.axis_index("vec")
    prev, nxt = lax.rem(lat + LAT - 1, LAT), lax.rem(lat + 1, LAT)
    y = lax.rem(vec, NY)
    base = vec - y
    partner = lax.rem(vec + NY, VEC)

    def y_peer(d):
        return base + lax.rem(y + d, NY)

    load = pltpu.make_async_copy(x_hbm, xv, xsem)
    load.start()

    barrier = pltpu.get_barrier_semaphore()
    for to in (prev, nxt):
        pl.semaphore_signal(barrier, 1, device_id={"lat": to}, device_id_type=MESH)
    for to in (y_peer(1), y_peer(2), y_peer(3), partner):
        pl.semaphore_signal(barrier, 1, device_id={"vec": to}, device_id_type=MESH)

    c0, c1, c2, c3, c4 = (coef[k] for k in range(5))
    h = inverse_bound
    a0 = c0 - c2 + c4
    a1 = (3.0 * c3 - c1) * h
    a2 = (2.0 * c2 - 8.0 * c4) * (h * h)
    a3 = c3 * (-4.0 * h * h * h)
    a4 = c4 * (8.0 * h * h * h * h)

    by_deal = deal()
    for q in range(4):
        cols = slice(q * 256, (q + 1) * 256)
        SP[:, cols] = permuted(s_vmem[:, :, cols].reshape(3 * ROWS, 256), by_deal)
    for c in range(3):
        for k in range(2):
            q, at = 2 * c + k, c * ROWS + k
            SHs[0, q : q + 1, :] = SP[at : at + 1, :]
            SHs[1, q : q + 1, :] = SP[at + 14 : at + 15, :]
    for s in range(2):
        SHs[s, 6:8, :] = jnp.zeros((2, COLS), jnp.float32)
    zero = jnp.zeros((8, COLS), jnp.float32)
    for row in range(ROWS):
        for c in range(3):
            at = c * ROWS + row
            SB[PAD + row, c] = jnp.broadcast_to(2.0 * SP[at : at + 1, :], (8, COLS))

    def swap(order):
        n = 16 * len(order)
        m = lax.broadcasted_iota(jnp.int32, (n, 256), 0)
        k = lax.broadcasted_iota(jnp.int32, (n, 256), 1)
        at = m // 16
        row = jnp.where(at < 2, at, at + 12) if order[0] == 0 else at + 2
        return jnp.where((k % 16 == row) & (k // 16 == m % 16), 1.0, 0.0).astype(jnp.bfloat16)

    def spread(order):
        by = swap(order)

        @pl.loop(0, 4)
        def _(c):
            for q in range(4):
                cols = slice(q * 256, (q + 1) * 256)
                got = jnp.dot(
                    by, xv[c, :, :, cols].reshape(256, 256), preferred_element_type=jnp.float32
                ).astype(jnp.bfloat16)
                got = jnp.dot(got, by_deal, preferred_element_type=jnp.float32)
                for at, row in enumerate(order):
                    for g in range(2):
                        lo = at * 16 + g * 8
                        R[g, PAD + row, c, :, cols] = got[lo : lo + 8]

    load.wait()
    spread((0, 1, 14, 15))
    pl.semaphore_wait(barrier, 2 + 4)

    def spin_copy(s):
        return pltpu.make_async_remote_copy(
            SHs.at[s], SHr.at[1 - s], ss.at[s], sr.at[1 - s],
            device_id={"lat": (prev, nxt)[s]}, device_id_type=MESH,
        )

    def halo_copy(s, g):
        src, dst = ((4, 20), (18, 2))[s]
        return pltpu.make_async_remote_copy(
            R.at[g, pl.ds(src, 2)], R.at[g, pl.ds(dst, 2)], hs.at[s, g], hr.at[1 - s, g],
            device_id={"lat": (prev, nxt)[s]}, device_id_type=MESH,
        )

    for s in range(2):
        spin_copy(s).start()
    for g in range(2):
        for s in range(2):
            halo_copy(s, g).start()

    spread(tuple(range(2, 14)))
    for c in range(3):
        for row in (1, 22):
            SB[row, c] = zero
    for g in range(2):
        for row in (0, 1, 22, 23):
            for c in range(4):
                R[g, row, c] = zero
        for s in range(2):
            for j in range(BLOCKS):
                E[s, g, j, 48:64, :] = jnp.zeros((16, 128), jnp.float32)

    lane = lax.broadcasted_iota(jnp.int32, (8, 128), 1)
    first, last = lane == 0, lane == 127

    def around(ref, at, j):
        other = ref[at + (slice(None), lanes(j ^ 1))]
        if j % 2 == 0:
            return other + pltpu.roll(
                jnp.where(last, ref[at + (slice(None), lanes(j - 1))], other), 1, 1
            )
        return other + pltpu.roll(
            jnp.where(first, ref[at + (slice(None), lanes(j + 1))], other), 127, 1
        )

    def hop(src, g, row, j):
        cols = (slice(None), lanes(j))
        spin = [SB[(PAD + row, c) + cols] for c in range(3)]
        state = [src[(g, PAD + row, c) + cols] for c in range(4)]
        onsite = spin_on(state, spin)
        res = []
        for c in range(4):
            n = src[(g, PAD + row - 1, c) + cols] + src[(g, PAD + row + 1, c) + cols]
            res.append((n + around(src, (g, PAD + row, c), j)) - onsite[c])
        return res

    def steps(groups, start, count, body):
        each = STEPS_EACH // len(groups)

        @pl.loop(0, count // each)
        def _(i):
            for k in range(each):
                for g in groups:
                    body(g, start + each * i + k)

    def sweep(groups, starts, counts, keep):
        def third(g, row):
            for j in range(BLOCKS):
                cols = (slice(None), lanes(j))
                got = hop(R, g, row, j)
                for c in range(4):
                    W3[(g, PAD + row, c) + cols] = a4 * got[c] + a3 * R[(g, PAD + row, c) + cols]

        steps(groups, starts[0], counts[0], third)

        for level, (src, dst, a) in enumerate(((W3, W2, a2), (W2, W1, a1)), 1):
            def lower(g, row):
                for j in range(BLOCKS):
                    cols = (slice(None), lanes(j))
                    got = hop(src, g, row, j)
                    for c in range(4):
                        dst[(g, PAD + row, c) + cols] = got[c] + a * R[(g, PAD + row, c) + cols]

            steps(groups, starts[level], counts[level], lower)

        def finish(g, row):
            for j in range(BLOCKS):
                cols = (slice(None), lanes(j))
                got = hop(W1, g, row, j)
                r = [R[(g, PAD + row, c) + cols] for c in range(4)]
                w = [got[c] + a0 * r[c] for c in range(4)]
                for c, d in enumerate(density(r, w)):
                    keep(g, c, j, row, d)

        steps(groups, starts[3], counts[3], finish)

    def fold(ref, at):
        parts = []
        for g in range(2):
            for s in range(8):
                parts.append(ref[at(g) + (pl.ds(s, 8, stride=8), slice(None))])
        while len(parts) > 1:
            parts = [parts[i] + parts[i + 1] for i in range(0, len(parts), 2)]
        return parts[0]

    def refs(grp, mid, edge):
        return mid if grp is None else edge.at[grp]

    def sem(ref, grp, *at):
        return ref.at[(0 if grp is None else 1 + grp, *at)]

    def y_scatter(grp, d):
        to = y_peer(d)
        return pltpu.make_async_remote_copy(
            refs(grp, FM, FE).at[to - base], refs(grp, RM, RE).at[d],
            sem(ys_s, grp, d), sem(ys_r, grp, d),
            device_id={"vec": to}, device_id_type=MESH,
        )

    def x_exchange(grp):
        return pltpu.make_async_remote_copy(
            refs(grp, QM, QE), refs(grp, XM, XE), sem(xs_s, grp), sem(xs_r, grp),
            device_id={"vec": partner}, device_id_type=MESH,
        )

    def y_gather(grp, d):
        here = refs(grp, out_mid, out_edge).at[y]
        return pltpu.make_async_remote_copy(
            here, here, sem(yg_s, grp, d), sem(yg_r, grp, d),
            device_id={"vec": y_peer(d)}, device_id_type=MESH,
        )

    def scatter(grp):
        for d in range(1, NY):
            y_scatter(grp, d).start()

    def exchange(grp):
        for d in range(1, NY):
            y_scatter(grp, d).wait_recv()
        got, mine = refs(grp, RM, RE), refs(grp, FM, FE)
        total = (mine[y] + got[1]) + (got[2] + got[3])
        into = refs(grp, QM, QE)
        if grp is None:
            into[...] = total
        else:
            for d in range(NY):
                chip_push(d).wait_recv()
            extra = placed(grp, NY)
            for c in range(3):
                into[c] = total[c] + extra[c]
        x_exchange(grp).start()

    def gather(grp):
        x_exchange(grp).wait_recv()
        refs(grp, out_mid, out_edge)[y] = refs(grp, QM, QE)[...] + refs(grp, XM, XE)[...]
        for d in range(1, NY):
            y_gather(grp, d).start()

    def keep_mid(g, c, j, row, d):
        at = pl.multiple_of((row - 4) * 8, 8)
        DM[g, c, j, pl.ds(at, 8), :] = d

    def keep_edge(s):
        def keep(g, c, j, row, d):
            at = pl.multiple_of(lax.rem(row + 2 * s, 4) * 8 + 32 * (j % 2), 8)
            DE[s, g, c, j // 2, pl.ds(at, 8), :] = d

        return keep

    sweep((0, 1), (1, 2, 3, 4), (14, 12, 10, 8), keep_mid)

    @pl.loop(0, NY)
    def _(q):
        for half in range(2):
            for c in range(3):
                FM[q, half, c] = fold(DM, lambda g: (g, c, 2 * q + half))

    scatter(None)

    for s in range(2):
        spin_copy(s).wait()
    for s in range(2):
        for c in range(3):
            for k in range(2):
                q = 2 * c + k
                SB[(2, 20)[s] + k, c] = jnp.broadcast_to(2.0 * SHr[s, q : q + 1, :], (8, COLS))

    def push(s, g):
        far, near = 2 + 11 * s + PAD, PAD - 1 + 17 * s
        row_far, row_next = PAD - 2 + 19 * s, PAD + 3 + 9 * s
        low = PAD - 1 + 14 * s
        at0 = [pl.multiple_of((2 * c + 1 - s) * 8, 8) for c in range(3)]
        at1 = [pl.multiple_of((2 * c + s) * 8, 8) for c in range(3)]
        for j in range(BLOCKS):
            cols = (slice(None), lanes(j))
            spin = [
                (SB[(low, c) + cols] + SB[(low + 1, c) + cols])
                + (SB[(low + 2, c) + cols] + SB[(low + 3, c) + cols])
                for c in range(3)
            ]
            b2 = [R[(g, far, c) + cols] for c in range(4)]
            onsite = spin_on(b2, spin)
            u, v = [], []
            for c in range(4):
                more = R[(g, row_next, c) + cols] + 4.0 * around(R, (g, far, c), j)
                u.append(a3 * b2[c] + a4 * (more - onsite[c]))
                v.append(a4 * b2[c])
            r0 = [R[(g, near, c) + cols] for c in range(4)]
            r1 = [R[(g, row_far, c) + cols] for c in range(4)]
            for c, d in enumerate(density(r0, u)):
                E[s, g, j, pl.ds(at0[c], 8), :] = d
            for c, d in enumerate(density(r1, v)):
                E[s, g, j, pl.ds(at1[c], 8), :] = d

    def wait_halo(s, g):
        pltpu.make_async_copy(R.at[g, pl.ds(2, 2)], R.at[g, pl.ds(2, 2)], hr.at[s, g]).wait()

    chip_side = 1 - lax.rem(lat, 2)
    link_side = 1 - chip_side

    def beyond(s):
        return lax.rem(lat + LAT - 1 + 2 * s, LAT)

    def chip_push(d):
        to = y_peer(d)
        return pltpu.make_async_remote_copy(
            PBs.at[chip_side, pl.ds(2 * (to - base), 2)], PBr.at[1 - chip_side, d],
            ps.at[0, d], pr.at[0, d],
            device_id={"lat": beyond(chip_side), "vec": to}, device_id_type=MESH,
        )

    def link_push(d):
        to = lax.rem(vec + d, VEC)
        return pltpu.make_async_remote_copy(
            PBs.at[link_side, pl.ds(2 * lax.rem(to, NY), 2)], PBr.at[1 - link_side, d],
            ps.at[1, d], pr.at[1, d],
            device_id={"lat": beyond(link_side), "vec": to}, device_id_type=MESH,
        )

    def link_scatter(d):
        to = lax.rem(vec + d, VEC)
        return pltpu.make_async_remote_copy(
            FE.at[link_side, lax.rem(to, NY)], RB.at[d], bs_s.at[d], bs_r.at[d],
            device_id={"vec": to}, device_id_type=MESH,
        )

    sub = lax.broadcasted_iota(jnp.int32, (8, 128), 0)

    def placed(s, count):
        got = PBr[s, 0]
        for d in range(1, count):
            got = got + PBr[s, d]
        res = []
        for c in range(3):
            total = jnp.zeros((8, 128), jnp.float32)
            for half in range(2):
                here = (sub == 4 * half) | (sub == 4 * half + 1)
                moved = pltpu.roll(got[half], (4 * half - 2 * c) % 8, 0)
                total = jnp.where(here, moved, total)
            res.append(total)
        return res

    def wedge(s, groups):
        sweep(
            groups, (18 * s - 3, 16 * s - 2, 14 * s - 1, 12 * s), (4, 4, 4, 4), keep_edge(s)
        )

    def fold_push(s):
        @pl.loop(0, BLOCKS)
        def _(j):
            PBs[s, j] = fold(E, lambda g: (s, g, j))

    def fold_edge(s):
        @pl.loop(0, NY)
        def _(q):
            for c in range(3):
                FE[s, q, c] = fold(DE, lambda g: (s, g, c, q))

    s = chip_side
    for g in range(2):
        wait_halo(s, g)
    wedge(s, (0, 1))
    exchange(None)
    for g in range(2):
        push(s, g)
    fold_push(s)
    for d in range(NY):
        chip_push(d).start()
    fold_edge(s)
    scatter(s)

    s = link_side
    wait_halo(s, 0)
    push(s, 0)
    wedge(s, (0,))
    gather(None)
    exchange(chip_side)
    wait_halo(s, 1)
    push(s, 1)
    fold_push(s)
    for d in range(VEC):
        link_push(d).start()
    wedge(s, (1,))
    fold_edge(s)
    for d in range(1, VEC):
        link_scatter(d).start()
    gather(chip_side)
    for d in range(1, VEC):
        link_scatter(d).wait_recv()
    for d in range(VEC):
        link_push(d).wait_recv()
    extra = placed(s, VEC)
    for c in range(3):
        total = FE[s, y, c] + extra[c]
        for d in range(1, VEC):
            total = total + RB[d, c]
        out_edge[s, y, c] = total
    for d in range(1, NY):
        y_gather(s, d).start()

    for s in range(2):
        for g in range(2):
            halo_copy(s, g).wait_send()
    for d in range(NY):
        chip_push(d).wait_send()
    for d in range(VEC):
        link_push(d).wait_send()
    for d in range(1, VEC):
        link_scatter(d).wait_send()
    for grp in (None, chip_side):
        x_exchange(grp).wait_send()
        for d in range(1, NY):
            y_scatter(grp, d).wait_send()
            y_gather(grp, d).wait()
    for d in range(1, NY):
        y_gather(link_side, d).wait()


def rotate_kernel(mid_ref, edge_ref, s_ref, rot, fields):
    sub = lax.broadcasted_iota(jnp.int32, (8, 128), 0)
    top, third = sub < 4, sub < 6
    by = deal(inverse=True)
    dealt = [[] for _ in range(BLOCKS)]
    for j in range(BLOCKS):
        q, half = divmod(j, 2)
        low, high = [], []
        for c in range(3):
            mid = pltpu.roll(mid_ref[q, half, c], 4, 0)
            start, end = edge_ref[0, q, c], edge_ref[1, q, c]
            if half:
                start = pltpu.roll(start, 4, 0)
            end = jnp.where(
                third,
                pltpu.roll(end, (2 - 4 * half) % 8, 0),
                pltpu.roll(end, (6 - 4 * half) % 8, 0),
            )
            low.append(jnp.where(top, start, mid))
            high.append(jnp.where(top, mid, end))
        dealt[j] = jnp.concatenate(low + high, axis=0) * (coupling / (VECS * VEC))
    for j in range(BLOCKS):
        if j % 2 == 0:
            natural = permuted(jnp.concatenate(dealt[j : j + 2], axis=1), by)
        cols = lanes(j)
        for block in range(2):
            rows = slice(block * 8, block * 8 + 8)
            at = (j % 2) * 128
            B = [
                natural[(3 * block + c) * 8 : (3 * block + c + 1) * 8, at : at + 128]
                for c in range(3)
            ]
            S = [s_ref[c, rows, cols] for c in range(3)]
            square = B[0] * B[0] + B[1] * B[1] + B[2] * B[2]
            size = jnp.sqrt(square)
            half_angle = 0.5 * size
            sin_h, cos_h = jnp.sin(half_angle), jnp.cos(half_angle)
            some = size > 0.0
            safe = jnp.where(some, size, 1.0)
            ratio = jnp.where(some, sin_h / safe, 0.5)
            cosine = 1.0 - 2.0 * (sin_h * sin_h)
            sine_ratio = 2.0 * (ratio * cos_h)
            along = 2.0 * (ratio * ratio) * (B[0] * S[0] + B[1] * S[1] + B[2] * S[2])
            cross = (
                B[1] * S[2] - B[2] * S[1],
                B[2] * S[0] - B[0] * S[2],
                B[0] * S[1] - B[1] * S[0],
            )
            for c in range(3):
                fields[c, rows, cols] = B[c]
                rot[c, rows, cols] = (cosine * S[c] + sine_ratio * cross[c]) + along * B[c]


def shards(vectors, classical_spins, coefficients):
    f32 = jnp.float32
    vmem = pl.BlockSpec(memory_space=pltpu.VMEM)
    dma = pltpu.SemaphoreType.DMA
    mid, edge = (NY, 2, 3, 8, 128), (2, NY, 3, 8, 128)
    parts = pl.pallas_call(
        field_kernel,
        name="fields",
        out_shape=(jax.ShapeDtypeStruct(mid, f32), jax.ShapeDtypeStruct(edge, f32)),
        in_specs=[
            pl.BlockSpec(memory_space=pltpu.SMEM),
            pl.BlockSpec(memory_space=pl.ANY),
            vmem,
        ],
        out_specs=(vmem, vmem),
        scratch_shapes=[
            pltpu.VMEM((4, VECS, ROWS, COLS), jnp.bfloat16),
            *[pltpu.VMEM((2, 24, 4, 8, COLS), f32)] * 4,
            pltpu.VMEM((24, 3, 8, COLS), f32),
            pltpu.VMEM((2, 8, COLS), f32),
            pltpu.VMEM((2, 8, COLS), f32),
            pltpu.VMEM((2, 3, BLOCKS, 64, 128), f32),
            pltpu.VMEM((2, 2, 3, NY, 64, 128), f32),
            pltpu.VMEM((2, 2, BLOCKS, 64, 128), f32),
            pltpu.VMEM((2, BLOCKS, 8, 128), f32),
            pltpu.VMEM((2, VEC, 2, 8, 128), f32),
            pltpu.VMEM(mid, f32), pltpu.VMEM(mid, f32),
            pltpu.VMEM(mid[1:], f32), pltpu.VMEM(mid[1:], f32),
            pltpu.VMEM(edge, f32), pltpu.VMEM(edge, f32),
            pltpu.VMEM((2, 3, 8, 128), f32), pltpu.VMEM((2, 3, 8, 128), f32),
            pltpu.VMEM((3 * ROWS, COLS), f32),
            pltpu.VMEM((VEC, 3, 8, 128), f32),
            dma, dma((2, 2)), dma((2, 2)), dma((2,)), dma((2,)), dma((2, VEC)), dma((2, VEC)),
            dma((3, NY)), dma((3, NY)), dma((3,)), dma((3,)), dma((3, NY)), dma((3, NY)),
            dma((VEC,)), dma((VEC,)),
        ],
        compiler_params=pltpu.CompilerParams(
            collective_id=0, has_side_effects=True, vmem_limit_bytes=60 << 20
        ),
    )(coefficients, vectors, classical_spins)
    out = jax.ShapeDtypeStruct((3, ROWS, COLS), f32)
    rotated, fields = pl.pallas_call(
        rotate_kernel,
        name="rotate",
        out_shape=(out, out),
        in_specs=[vmem, vmem, vmem],
        out_specs=(vmem, vmem),
    )(*parts, classical_spins)
    return rotated, fields


def solution(mesh):
    placed = (P(None, "vec", "lat", None), P(None, "lat", None), P())
    return jax.shard_map(
        shards,
        mesh=mesh,
        in_specs=placed,
        out_specs=(P(None, "lat", None), P(None, "lat", None)),
        check_vma=False,
    )
```

```python
import functools

import jax
import jax.numpy as jnp
from jax import lax
from jax.experimental import pallas as pl
from jax.experimental.pallas import tpu as pltpu
from jax.sharding import PartitionSpec as P

MESH = pl.DeviceIdType.MESH
LAT, VEC, NY = 16, 8, 4
ROWS, COLS, VECS = 16, 1024, 16
BLOCKS = COLS // 128
PAD = 4
STEPS_EACH = 4
coupling = 2.0
inverse_bound = 1.0 / 6.5


def spin_on(state, spin):
    x, y, z = spin
    p0, p1, p2, p3 = state
    return (
        (z * p0 + x * p2) + y * p3,
        (z * p1 + x * p3) - y * p2,
        (x * p0 - y * p1) - z * p2,
        (x * p1 + y * p0) - z * p3,
    )


def density(r, w):
    return (
        (r[0] * w[2] + r[1] * w[3]) + (r[2] * w[0] + r[3] * w[1]),
        (r[0] * w[3] - r[1] * w[2]) - (r[2] * w[1] - r[3] * w[0]),
        (r[0] * w[0] + r[1] * w[1]) - (r[2] * w[2] + r[3] * w[3]),
    )


def bf16_parts(x):
    high = x.astype(jnp.bfloat16)
    rest = x - high.astype(jnp.float32)
    mid = rest.astype(jnp.bfloat16)
    low = (rest - mid.astype(jnp.float32)).astype(jnp.bfloat16)
    return jnp.concatenate([high, mid, low], axis=0)


def permuted(x, by):
    n = x.shape[0]
    got = jnp.dot(bf16_parts(x), by, preferred_element_type=jnp.float32)
    return (got[:n] + got[n : 2 * n]) + got[2 * n :]


def deal(inverse=False):
    here = lax.broadcasted_iota(jnp.int32, (256, 256), int(inverse))
    there = lax.broadcasted_iota(jnp.int32, (256, 256), int(not inverse))
    source = jnp.where(there < 128, 2 * there, 2 * there - 255)
    return jnp.where(here == source, 1.0, 0.0).astype(jnp.bfloat16)


def lanes(j):
    j = j % BLOCKS
    return slice(j * 128, (j + 1) * 128)


def field_kernel(
    coef, x_hbm, s_hbm, out_mid, out_edge,
    xv, s_vmem, R, W3, W2, W1, SB, SHs, SHr, DM, DE, E, PBs, PBr,
    FM, RM, QM, XM, FE, RE, QE, XE, SP, GX,
    xsem, ssem, hs, hr, ss, sr, ps, pr, ys_s, ys_r, xs_s, xs_r, yg_s, yg_r, bs_s, bs_r,
):
    lat, vec = lax.axis_index("lat"), lax.axis_index("vec")
    prev, nxt = lax.rem(lat + LAT - 1, LAT), lax.rem(lat + 1, LAT)
    y = lax.rem(vec, NY)
    base = vec - y
    partner = lax.rem(vec + NY, VEC)

    def y_peer(d):
        return base + lax.rem(y + d, NY)

    load_spins = pltpu.make_async_copy(s_hbm, s_vmem, ssem)
    load_spins.start()
    load = pltpu.make_async_copy(x_hbm, xv, xsem)
    load.start()

    barrier = pltpu.get_barrier_semaphore()
    for to in (prev, nxt):
        pl.semaphore_signal(barrier, 1, device_id={"lat": to}, device_id_type=MESH)
    for to in (y_peer(1), y_peer(2), y_peer(3), partner):
        pl.semaphore_signal(barrier, 1, device_id={"vec": to}, device_id_type=MESH)

    c0, c1, c2, c3, c4 = (coef[k] for k in range(5))
    h = inverse_bound
    a0 = c0 - c2 + c4
    a1 = (3.0 * c3 - c1) * h
    a2 = (2.0 * c2 - 8.0 * c4) * (h * h)
    a3 = c3 * (-4.0 * h * h * h)
    a4 = c4 * (8.0 * h * h * h * h)

    by_deal = deal()

    def swap(order):
        n = 16 * len(order)
        m = lax.broadcasted_iota(jnp.int32, (n, 256), 0)
        k = lax.broadcasted_iota(jnp.int32, (n, 256), 1)
        at = m // 16
        row = jnp.where(at < 2, at, at + 12) if order[0] == 0 else at + 2
        return jnp.where((k % 16 == row) & (k // 16 == m % 16), 1.0, 0.0).astype(jnp.bfloat16)

    def spread(order):
        by = swap(order)

        @pl.loop(0, 4)
        def _(c):
            for q in range(4):
                cols = slice(q * 256, (q + 1) * 256)
                got = jnp.dot(
                    by, xv[c, :, :, cols].reshape(256, 256), preferred_element_type=jnp.float32
                ).astype(jnp.bfloat16)
                got = jnp.dot(got, by_deal, preferred_element_type=jnp.float32)
                for at, row in enumerate(order):
                    for g in range(2):
                        lo = at * 16 + g * 8
                        R[g, PAD + row, c, :, cols] = got[lo : lo + 8]

    def spin_copy(s):
        return pltpu.make_async_remote_copy(
            SHs.at[s], SHr.at[1 - s], ss.at[s], sr.at[1 - s],
            device_id={"lat": (prev, nxt)[s]}, device_id_type=MESH,
        )

    def halo_copy(s, g):
        src, dst = ((4, 20), (18, 2))[s]
        return pltpu.make_async_remote_copy(
            R.at[g, pl.ds(src, 2)], R.at[g, pl.ds(dst, 2)], hs.at[s, g], hr.at[1 - s, g],
            device_id={"lat": (prev, nxt)[s]}, device_id_type=MESH,
        )

    load_spins.wait()
    for c in range(3):
        for k in range(2):
            q = 2 * c + k
            SHs[0, q : q + 1, :] = s_vmem[c, k : k + 1, :]
            SHs[1, q : q + 1, :] = s_vmem[c, 14 + k : 15 + k, :]
    for s in range(2):
        SHs[s, 6:8, :] = jnp.zeros((2, COLS), jnp.float32)
    load.wait()
    spread((0, 1, 14, 15))
    pl.semaphore_wait(barrier, 2 + 4)
    for s in range(2):
        spin_copy(s).start()
    for g in range(2):
        for s in range(2):
            halo_copy(s, g).start()

    for q in range(4):
        cols = slice(q * 256, (q + 1) * 256)
        SP[:, cols] = permuted(s_vmem[:, :, cols].reshape(3 * ROWS, 256), by_deal)
    zero = jnp.zeros((8, COLS), jnp.float32)
    for row in range(ROWS):
        for c in range(3):
            at = c * ROWS + row
            SB[PAD + row, c] = jnp.broadcast_to(2.0 * SP[at : at + 1, :], (8, COLS))

    spread(tuple(range(2, 14)))
    for c in range(3):
        for row in (1, 22):
            SB[row, c] = zero
    for g in range(2):
        for row in (0, 1, 22, 23):
            for c in range(4):
                R[g, row, c] = zero
        for s in range(2):
            for j in range(BLOCKS):
                E[s, g, j, 48:64, :] = jnp.zeros((16, 128), jnp.float32)

    lane = lax.broadcasted_iota(jnp.int32, (8, 128), 1)
    first, last = lane == 0, lane == 127

    def around(ref, at, j):
        other = ref[at + (slice(None), lanes(j ^ 1))]
        if j % 2 == 0:
            return other + pltpu.roll(
                jnp.where(last, ref[at + (slice(None), lanes(j - 1))], other), 1, 1
            )
        return other + pltpu.roll(
            jnp.where(first, ref[at + (slice(None), lanes(j + 1))], other), 127, 1
        )

    def hop(src, g, row, j):
        cols = (slice(None), lanes(j))
        spin = [SB[(PAD + row, c) + cols] for c in range(3)]
        state = [src[(g, PAD + row, c) + cols] for c in range(4)]
        onsite = spin_on(state, spin)
        res = []
        for c in range(4):
            n = src[(g, PAD + row - 1, c) + cols] + src[(g, PAD + row + 1, c) + cols]
            res.append((n + around(src, (g, PAD + row, c), j)) - onsite[c])
        return res

    def steps(groups, start, count, body):
        each = 2

        @pl.loop(0, count // each)
        def _(i):
            for k in range(each):
                for g in groups:
                    body(g, start + each * i + k)

    def sweep(groups, starts, counts, keep):
        def third(g, row):
            for j in range(BLOCKS):
                cols = (slice(None), lanes(j))
                got = hop(R, g, row, j)
                for c in range(4):
                    W3[(g, PAD + row, c) + cols] = a4 * got[c] + a3 * R[(g, PAD + row, c) + cols]

        steps(groups, starts[0], counts[0], third)

        for level, (src, dst, a) in enumerate(((W3, W2, a2), (W2, W1, a1)), 1):
            def lower(g, row):
                for j in range(BLOCKS):
                    cols = (slice(None), lanes(j))
                    got = hop(src, g, row, j)
                    for c in range(4):
                        dst[(g, PAD + row, c) + cols] = got[c] + a * R[(g, PAD + row, c) + cols]

            steps(groups, starts[level], counts[level], lower)

        def finish(g, row):
            for j in range(BLOCKS):
                cols = (slice(None), lanes(j))
                got = hop(W1, g, row, j)
                r = [R[(g, PAD + row, c) + cols] for c in range(4)]
                w = [got[c] + a0 * r[c] for c in range(4)]
                for c, d in enumerate(density(r, w)):
                    keep(g, c, j, row, d)

        steps(groups, starts[3], counts[3], finish)

    def fold(ref, at):
        parts = []
        for g in range(2):
            for s in range(8):
                parts.append(ref[at(g) + (pl.ds(s, 8, stride=8), slice(None))])
        while len(parts) > 1:
            parts = [parts[i] + parts[i + 1] for i in range(0, len(parts), 2)]
        return parts[0]

    def refs(grp, mid, edge):
        return mid if grp is None else edge.at[grp]

    def sem(ref, grp, *at):
        return ref.at[(0 if grp is None else 1 + grp, *at)]

    def y_scatter(grp, d):
        to = y_peer(d)
        return pltpu.make_async_remote_copy(
            refs(grp, FM, FE).at[to - base], refs(grp, RM, RE).at[d],
            sem(ys_s, grp, d), sem(ys_r, grp, d),
            device_id={"vec": to}, device_id_type=MESH,
        )

    def x_exchange(grp):
        return pltpu.make_async_remote_copy(
            refs(grp, QM, QE), refs(grp, XM, XE), sem(xs_s, grp), sem(xs_r, grp),
            device_id={"vec": partner}, device_id_type=MESH,
        )

    def y_gather(grp, d):
        here = refs(grp, out_mid, out_edge).at[y]
        return pltpu.make_async_remote_copy(
            here, here, sem(yg_s, grp, d), sem(yg_r, grp, d),
            device_id={"vec": y_peer(d)}, device_id_type=MESH,
        )

    def scatter(grp):
        for d in range(1, NY):
            y_scatter(grp, d).start()

    def partial_sum(grp):
        for d in range(1, NY):
            y_scatter(grp, d).wait_recv()
        got, mine = refs(grp, RM, RE), refs(grp, FM, FE)
        return (mine[y] + got[1]) + (got[2] + got[3])

    def edge_partial_sum(s, which, into):
        total = partial_sum(s)
        for d in range(NY):
            push_copy(s, which, d).wait_recv()
        extra = placed(s)
        for c in range(3):
            into[c] = total[c] + extra[c]

    def exchange(grp):
        if grp is None:
            QM[...] = partial_sum(grp)
        else:
            edge_partial_sum(grp, 0, QE.at[grp])
        x_exchange(grp).start()

    def gather(grp):
        x_exchange(grp).wait_recv()
        refs(grp, out_mid, out_edge)[y] = refs(grp, QM, QE)[...] + refs(grp, XM, XE)[...]
        for d in range(1, NY):
            y_gather(grp, d).start()

    def keep_mid(g, c, j, row, d):
        at = pl.multiple_of((row - 4) * 8, 8)
        DM[g, c, j, pl.ds(at, 8), :] = d

    def keep_edge(s):
        def keep(g, c, j, row, d):
            at = pl.multiple_of(lax.rem(row + 2 * s, 4) * 8 + 32 * (j % 2), 8)
            DE[s, g, c, j // 2, pl.ds(at, 8), :] = d

        return keep

    sweep((0, 1), (1, 2, 3, 4), (14, 12, 10, 8), keep_mid)

    @pl.loop(0, NY)
    def _(q):
        for half in range(2):
            for c in range(3):
                FM[q, half, c] = fold(DM, lambda g: (g, c, 2 * q + half))

    scatter(None)

    for s in range(2):
        spin_copy(s).wait_recv()
    for q in range(4):
        cols = slice(q * 256, (q + 1) * 256)
        got = 2.0 * permuted(SHr[:, :, cols].reshape(16, 256), by_deal)
        for s in range(2):
            for c in range(3):
                for k in range(2):
                    at = 8 * s + 2 * c + k
                    SB[(2, 20)[s] + k, c, :, cols] = jnp.broadcast_to(
                        got[at : at + 1], (8, 256)
                    )

    def push(s, g):
        far, near = 2 + 11 * s + PAD, PAD - 1 + 17 * s
        row_far, row_next = PAD - 2 + 19 * s, PAD + 3 + 9 * s
        low = PAD - 1 + 14 * s
        at0 = [pl.multiple_of((2 * c + 1 - s) * 8, 8) for c in range(3)]
        at1 = [pl.multiple_of((2 * c + s) * 8, 8) for c in range(3)]
        for j in range(BLOCKS):
            cols = (slice(None), lanes(j))
            spin = [
                (SB[(low, c) + cols] + SB[(low + 1, c) + cols])
                + (SB[(low + 2, c) + cols] + SB[(low + 3, c) + cols])
                for c in range(3)
            ]
            b2 = [R[(g, far, c) + cols] for c in range(4)]
            onsite = spin_on(b2, spin)
            u, v = [], []
            for c in range(4):
                more = R[(g, row_next, c) + cols] + 4.0 * around(R, (g, far, c), j)
                u.append(a3 * b2[c] + a4 * (more - onsite[c]))
                v.append(a4 * b2[c])
            r0 = [R[(g, near, c) + cols] for c in range(4)]
            r1 = [R[(g, row_far, c) + cols] for c in range(4)]
            for c, d in enumerate(density(r0, u)):
                E[s, g, j, pl.ds(at0[c], 8), :] = d
            for c, d in enumerate(density(r1, v)):
                E[s, g, j, pl.ds(at1[c], 8), :] = d

    def wait_halo(s, g):
        pltpu.make_async_copy(R.at[g, pl.ds(2, 2)], R.at[g, pl.ds(2, 2)], hr.at[s, g]).wait()

    chip_side = 1 - lax.rem(lat, 2)
    link_side = 1 - chip_side

    def beyond(s):
        return lax.rem(lat + LAT - 1 + 2 * s, LAT)

    def push_copy(s, which, d):
        to = y_peer(d)
        return pltpu.make_async_remote_copy(
            PBs.at[s, pl.ds(2 * (to - base), 2)], PBr.at[1 - s, d],
            ps.at[which, d], pr.at[which, d],
            device_id={"lat": beyond(s), "vec": to}, device_id_type=MESH,
        )

    def spread_sum(half, d):
        to = lax.rem(base + NY * half, VEC) + lax.rem(y + d, NY)
        return pltpu.make_async_remote_copy(
            GX.at[0, y], GX.at[half, y], bs_s.at[half, d], bs_r.at[half, d],
            device_id={"vec": to}, device_id_type=MESH,
        )

    others = [(0, 1), (0, 2), (0, 3), (1, 0), (1, 1), (1, 2), (1, 3)]

    sub = lax.broadcasted_iota(jnp.int32, (8, 128), 0)

    def placed(s):
        got = (PBr[s, 0] + PBr[s, 1]) + (PBr[s, 2] + PBr[s, 3])
        res = []
        for c in range(3):
            total = jnp.zeros((8, 128), jnp.float32)
            for half in range(2):
                here = (sub == 4 * half) | (sub == 4 * half + 1)
                moved = pltpu.roll(got[half], (4 * half - 2 * c) % 8, 0)
                total = jnp.where(here, moved, total)
            res.append(total)
        return res

    def wedge(s, groups):
        sweep(
            groups, (18 * s - 3, 16 * s - 2, 14 * s - 1, 12 * s), (4, 4, 4, 4), keep_edge(s)
        )

    def fold_push(s):
        @pl.loop(0, BLOCKS)
        def _(j):
            PBs[s, j] = fold(E, lambda g: (s, g, j))

    def fold_edge(s):
        @pl.loop(0, NY)
        def _(q):
            for c in range(3):
                FE[s, q, c] = fold(DE, lambda g: (s, g, c, q))

    s = chip_side
    for g in range(2):
        wait_halo(s, g)
    wedge(s, (0, 1))
    fold_edge(s)
    scatter(s)

    s = link_side
    wait_halo(s, 0)
    push(s, 0)
    wedge(s, (0,))
    exchange(None)
    for g in range(2):
        push(chip_side, g)
    fold_push(chip_side)
    for d in range(NY):
        push_copy(chip_side, 0, d).start()
    wait_halo(s, 1)
    push(s, 1)
    fold_push(s)
    for d in range(NY):
        push_copy(s, 1, d).start()
    wedge(s, (1,))
    fold_edge(s)
    scatter(s)
    exchange(chip_side)
    gather(None)
    edge_partial_sum(s, 1, GX.at[0, y])
    for half, d in others:
        spread_sum(half, d).start()
    gather(chip_side)

    for s in range(2):
        spin_copy(s).wait_send()
        for g in range(2):
            halo_copy(s, g).wait_send()
    for d in range(NY):
        push_copy(chip_side, 0, d).wait_send()
        push_copy(link_side, 1, d).wait_send()
    for d in range(1, NY):
        y_scatter(link_side, d).wait_send()
    for grp in (None, chip_side):
        x_exchange(grp).wait_send()
        for d in range(1, NY):
            y_scatter(grp, d).wait_send()
            y_gather(grp, d).wait()
    for half, d in others:
        spread_sum(half, d).wait()
    out_edge[link_side] = GX[0] + GX[1]


def rotate_kernel(mid_ref, edge_ref, s_ref, rot, fields):
    sub = lax.broadcasted_iota(jnp.int32, (8, 128), 0)
    top, third = sub < 4, sub < 6
    by = deal(inverse=True)
    dealt = [[] for _ in range(BLOCKS)]
    for j in range(BLOCKS):
        q, half = divmod(j, 2)
        low, high = [], []
        for c in range(3):
            mid = pltpu.roll(mid_ref[q, half, c], 4, 0)
            start, end = edge_ref[0, q, c], edge_ref[1, q, c]
            if half:
                start = pltpu.roll(start, 4, 0)
            end = jnp.where(
                third,
                pltpu.roll(end, (2 - 4 * half) % 8, 0),
                pltpu.roll(end, (6 - 4 * half) % 8, 0),
            )
            low.append(jnp.where(top, start, mid))
            high.append(jnp.where(top, mid, end))
        dealt[j] = jnp.concatenate(low + high, axis=0) * (coupling / (VECS * VEC))
    for j in range(BLOCKS):
        if j % 2 == 0:
            natural = permuted(jnp.concatenate(dealt[j : j + 2], axis=1), by)
        cols = lanes(j)
        for block in range(2):
            rows = slice(block * 8, block * 8 + 8)
            at = (j % 2) * 128
            B = [
                natural[(3 * block + c) * 8 : (3 * block + c + 1) * 8, at : at + 128]
                for c in range(3)
            ]
            S = [s_ref[c, rows, cols] for c in range(3)]
            square = B[0] * B[0] + B[1] * B[1] + B[2] * B[2]
            size = jnp.sqrt(square)
            half_angle = 0.5 * size
            sin_h, cos_h = jnp.sin(half_angle), jnp.cos(half_angle)
            some = size > 0.0
            safe = jnp.where(some, size, 1.0)
            ratio = jnp.where(some, sin_h / safe, 0.5)
            cosine = 1.0 - 2.0 * (sin_h * sin_h)
            sine_ratio = 2.0 * (ratio * cos_h)
            along = 2.0 * (ratio * ratio) * (B[0] * S[0] + B[1] * S[1] + B[2] * S[2])
            cross = (
                B[1] * S[2] - B[2] * S[1],
                B[2] * S[0] - B[0] * S[2],
                B[0] * S[1] - B[1] * S[0],
            )
            for c in range(3):
                fields[c, rows, cols] = B[c]
                rot[c, rows, cols] = (cosine * S[c] + sine_ratio * cross[c]) + along * B[c]


def shards(vectors, classical_spins, coefficients):
    f32 = jnp.float32
    vmem = pl.BlockSpec(memory_space=pltpu.VMEM)
    dma = pltpu.SemaphoreType.DMA
    mid, edge = (NY, 2, 3, 8, 128), (2, NY, 3, 8, 128)
    parts = pl.pallas_call(
        field_kernel,
        name="fields",
        out_shape=(jax.ShapeDtypeStruct(mid, f32), jax.ShapeDtypeStruct(edge, f32)),
        in_specs=[
            pl.BlockSpec(memory_space=pltpu.SMEM),
            pl.BlockSpec(memory_space=pl.ANY),
            pl.BlockSpec(memory_space=pl.ANY),
        ],
        out_specs=(vmem, vmem),
        scratch_shapes=[
            pltpu.VMEM((4, VECS, ROWS, COLS), jnp.bfloat16),
            pltpu.VMEM((3, ROWS, COLS), f32),
            *[pltpu.VMEM((2, 24, 4, 8, COLS), f32)] * 4,
            pltpu.VMEM((24, 3, 8, COLS), f32),
            pltpu.VMEM((2, 8, COLS), f32),
            pltpu.VMEM((2, 8, COLS), f32),
            pltpu.VMEM((2, 3, BLOCKS, 64, 128), f32),
            pltpu.VMEM((2, 2, 3, NY, 64, 128), f32),
            pltpu.VMEM((2, 2, BLOCKS, 64, 128), f32),
            pltpu.VMEM((2, BLOCKS, 8, 128), f32),
            pltpu.VMEM((2, NY, 2, 8, 128), f32),
            pltpu.VMEM(mid, f32), pltpu.VMEM(mid, f32),
            pltpu.VMEM(mid[1:], f32), pltpu.VMEM(mid[1:], f32),
            pltpu.VMEM(edge, f32), pltpu.VMEM(edge, f32),
            pltpu.VMEM((2, 3, 8, 128), f32), pltpu.VMEM((2, 3, 8, 128), f32),
            pltpu.VMEM((3 * ROWS, COLS), f32),
            pltpu.VMEM(edge, f32),
            dma, dma, dma((2, 2)), dma((2, 2)), dma((2,)), dma((2,)),
            dma((2, NY)), dma((2, NY)),
            dma((3, NY)), dma((3, NY)), dma((3,)), dma((3,)), dma((3, NY)), dma((3, NY)),
            dma((2, NY)), dma((2, NY)),
        ],
        compiler_params=pltpu.CompilerParams(
            collective_id=0, has_side_effects=True, vmem_limit_bytes=60 << 20
        ),
    )(coefficients, vectors, classical_spins)
    out = jax.ShapeDtypeStruct((3, ROWS, COLS), f32)
    rotated, fields = pl.pallas_call(
        rotate_kernel,
        name="rotate",
        out_shape=(out, out),
        in_specs=[vmem, vmem, vmem],
        out_specs=(vmem, vmem),
    )(*parts, classical_spins)
    return rotated, fields


def solution(mesh):
    placed = (P(None, "vec", "lat", None), P(None, "lat", None), P())
    return jax.shard_map(
        shards,
        mesh=mesh,
        in_specs=placed,
        out_specs=(P(None, "lat", None), P(None, "lat", None)),
        check_vma=False,
    )
```

```python
import functools

import jax
import jax.numpy as jnp
from jax import lax
from jax.experimental import pallas as pl
from jax.experimental.pallas import tpu as pltpu
from jax.sharding import PartitionSpec as P

MESH = pl.DeviceIdType.MESH
LAT, VEC, NY = 16, 8, 4
ROWS, COLS, VECS = 16, 1024, 16
BLOCKS = COLS // 128
PAD = 4
STEPS_EACH = 4
coupling = 2.0
inverse_bound = 1.0 / 6.5


def spin_on(state, spin):
    x, y, z = spin
    p0, p1, p2, p3 = state
    return (
        (z * p0 + x * p2) + y * p3,
        (z * p1 + x * p3) - y * p2,
        (x * p0 - y * p1) - z * p2,
        (x * p1 + y * p0) - z * p3,
    )


def density(r, w):
    return (
        (r[0] * w[2] + r[1] * w[3]) + (r[2] * w[0] + r[3] * w[1]),
        (r[0] * w[3] - r[1] * w[2]) - (r[2] * w[1] - r[3] * w[0]),
        (r[0] * w[0] + r[1] * w[1]) - (r[2] * w[2] + r[3] * w[3]),
    )


def bf16_parts(x):
    high = x.astype(jnp.bfloat16)
    rest = x - high.astype(jnp.float32)
    mid = rest.astype(jnp.bfloat16)
    low = (rest - mid.astype(jnp.float32)).astype(jnp.bfloat16)
    return jnp.concatenate([high, mid, low], axis=0)


def permuted(x, by):
    n = x.shape[0]
    got = jnp.dot(bf16_parts(x), by, preferred_element_type=jnp.float32)
    return (got[:n] + got[n : 2 * n]) + got[2 * n :]


def deal(inverse=False):
    here = lax.broadcasted_iota(jnp.int32, (256, 256), int(inverse))
    there = lax.broadcasted_iota(jnp.int32, (256, 256), int(not inverse))
    source = jnp.where(there < 128, 2 * there, 2 * there - 255)
    return jnp.where(here == source, 1.0, 0.0).astype(jnp.bfloat16)


def lanes(j):
    j = j % BLOCKS
    return slice(j * 128, (j + 1) * 128)


def field_kernel(
    coef, x_hbm, s_hbm, out_mid, out_edge,
    xv, s_vmem, R, W3, W2, W1, SB, SHs, SHr, DM, DE, E, PBs, PBr,
    FM, RM, QM, XM, FE, RE, QE, XE, SP, GX,
    xsem, ssem, hs, hr, ss, sr, ps, pr, ys_s, ys_r, xs_s, xs_r, yg_s, yg_r, bs_s, bs_r,
):
    lat, vec = lax.axis_index("lat"), lax.axis_index("vec")
    prev, nxt = lax.rem(lat + LAT - 1, LAT), lax.rem(lat + 1, LAT)
    y = lax.rem(vec, NY)
    base = vec - y
    partner = lax.rem(vec + NY, VEC)

    def y_peer(d):
        return base + lax.rem(y + d, NY)

    load_spins = pltpu.make_async_copy(s_hbm, s_vmem, ssem)
    load_spins.start()
    def load(g):
        half = (slice(None), pl.ds(8 * g, 8))
        return pltpu.make_async_copy(x_hbm.at[half], xv.at[half], xsem.at[g])

    load(0).start()
    load(1).start()

    barrier = pltpu.get_barrier_semaphore()
    for to in (prev, nxt):
        pl.semaphore_signal(barrier, 1, device_id={"lat": to}, device_id_type=MESH)
    for to in (y_peer(1), y_peer(2), y_peer(3), partner):
        pl.semaphore_signal(barrier, 1, device_id={"vec": to}, device_id_type=MESH)

    c0, c1, c2, c3, c4 = (coef[k] for k in range(5))
    h = inverse_bound
    a0 = c0 - c2 + c4
    a1 = (3.0 * c3 - c1) * h
    a2 = (2.0 * c2 - 8.0 * c4) * (h * h)
    a3 = c3 * (-4.0 * h * h * h)
    a4 = c4 * (8.0 * h * h * h * h)

    by_deal = deal()

    def swap(order):
        n = 16 * len(order)
        m = lax.broadcasted_iota(jnp.int32, (n, 256), 0)
        k = lax.broadcasted_iota(jnp.int32, (n, 256), 1)
        at = m // 16
        row = jnp.where(at < 2, at, at + 12) if order[0] == 0 else at + 2
        return jnp.where((k % 16 == row) & (k // 16 == m % 16), 1.0, 0.0).astype(jnp.bfloat16)

    def swap_ends():
        m = lax.broadcasted_iota(jnp.int32, (32, 128), 0)
        k = lax.broadcasted_iota(jnp.int32, (32, 128), 1)
        at = m // 8
        row = jnp.where(at < 2, at, at + 12)
        return jnp.where((k % 16 == row) & (k // 16 == m % 8), 1.0, 0.0).astype(jnp.bfloat16)

    def spread_ends(g, by):
        for c in range(4):
            for q in range(4):
                cols = slice(q * 256, (q + 1) * 256)
                got = jnp.dot(
                    by,
                    xv[c, 8 * g : 8 * g + 8, :, cols].reshape(128, 256),
                    preferred_element_type=jnp.float32,
                ).astype(jnp.bfloat16)
                got = jnp.dot(got, by_deal, preferred_element_type=jnp.float32)
                for at, row in enumerate((0, 1, 14, 15)):
                    R[g, PAD + row, c, :, cols] = got[8 * at : 8 * at + 8]

    def spread(order):
        by = swap(order)

        @pl.loop(0, 4)
        def _(c):
            for q in range(4):
                cols = slice(q * 256, (q + 1) * 256)
                got = jnp.dot(
                    by, xv[c, :, :, cols].reshape(256, 256), preferred_element_type=jnp.float32
                ).astype(jnp.bfloat16)
                got = jnp.dot(got, by_deal, preferred_element_type=jnp.float32)
                for at, row in enumerate(order):
                    for g in range(2):
                        lo = at * 16 + g * 8
                        R[g, PAD + row, c, :, cols] = got[lo : lo + 8]

    def spin_copy(s):
        return pltpu.make_async_remote_copy(
            SHs.at[s], SHr.at[1 - s], ss.at[s], sr.at[1 - s],
            device_id={"lat": (prev, nxt)[s]}, device_id_type=MESH,
        )

    def halo_copy(s, g):
        src, dst = ((4, 20), (18, 2))[s]
        return pltpu.make_async_remote_copy(
            R.at[g, pl.ds(src, 2)], R.at[g, pl.ds(dst, 2)], hs.at[s, g], hr.at[1 - s, g],
            device_id={"lat": (prev, nxt)[s]}, device_id_type=MESH,
        )

    load_spins.wait()
    for c in range(3):
        for k in range(2):
            q = 2 * c + k
            SHs[0, q : q + 1, :] = s_vmem[c, k : k + 1, :]
            SHs[1, q : q + 1, :] = s_vmem[c, 14 + k : 15 + k, :]
    for s in range(2):
        SHs[s, 6:8, :] = jnp.zeros((2, COLS), jnp.float32)
    by_ends = swap_ends()
    for g in range(2):
        load(g).wait()
        spread_ends(g, by_ends)
        if g == 0:
            pl.semaphore_wait(barrier, 2 + 4)
            for s in range(2):
                spin_copy(s).start()
        for s in range(2):
            halo_copy(s, g).start()

    for q in range(4):
        cols = slice(q * 256, (q + 1) * 256)
        SP[:, cols] = permuted(s_vmem[:, :, cols].reshape(3 * ROWS, 256), by_deal)
    zero = jnp.zeros((8, COLS), jnp.float32)
    for row in range(ROWS):
        for c in range(3):
            at = c * ROWS + row
            SB[PAD + row, c] = jnp.broadcast_to(2.0 * SP[at : at + 1, :], (8, COLS))

    spread(tuple(range(2, 14)))
    for c in range(3):
        for row in (1, 22):
            SB[row, c] = zero
    for g in range(2):
        for row in (0, 1, 22, 23):
            for c in range(4):
                R[g, row, c] = zero
        for s in range(2):
            for j in range(BLOCKS):
                E[s, g, j, 48:64, :] = jnp.zeros((16, 128), jnp.float32)

    lane = lax.broadcasted_iota(jnp.int32, (8, 128), 1)
    first, last = lane == 0, lane == 127

    def around(ref, at, j):
        other = ref[at + (slice(None), lanes(j ^ 1))]
        if j % 2 == 0:
            return other + pltpu.roll(
                jnp.where(last, ref[at + (slice(None), lanes(j - 1))], other), 1, 1
            )
        return other + pltpu.roll(
            jnp.where(first, ref[at + (slice(None), lanes(j + 1))], other), 127, 1
        )

    def hop(src, g, row, j):
        cols = (slice(None), lanes(j))
        spin = [SB[(PAD + row, c) + cols] for c in range(3)]
        state = [src[(g, PAD + row, c) + cols] for c in range(4)]
        onsite = spin_on(state, spin)
        res = []
        for c in range(4):
            n = src[(g, PAD + row - 1, c) + cols] + src[(g, PAD + row + 1, c) + cols]
            res.append((n + around(src, (g, PAD + row, c), j)) - onsite[c])
        return res

    def steps(groups, start, count, body):
        each = 2

        @pl.loop(0, count // each)
        def _(i):
            for k in range(each):
                for g in groups:
                    body(g, start + each * i + k)

    def sweep(groups, starts, counts, keep):
        def third(g, row):
            for j in range(BLOCKS):
                cols = (slice(None), lanes(j))
                got = hop(R, g, row, j)
                for c in range(4):
                    W3[(g, PAD + row, c) + cols] = a4 * got[c] + a3 * R[(g, PAD + row, c) + cols]

        steps(groups, starts[0], counts[0], third)

        for level, (src, dst, a) in enumerate(((W3, W2, a2), (W2, W1, a1)), 1):
            def lower(g, row):
                for j in range(BLOCKS):
                    cols = (slice(None), lanes(j))
                    got = hop(src, g, row, j)
                    for c in range(4):
                        dst[(g, PAD + row, c) + cols] = got[c] + a * R[(g, PAD + row, c) + cols]

            steps(groups, starts[level], counts[level], lower)

        def finish(g, row):
            for j in range(BLOCKS):
                cols = (slice(None), lanes(j))
                got = hop(W1, g, row, j)
                r = [R[(g, PAD + row, c) + cols] for c in range(4)]
                w = [got[c] + a0 * r[c] for c in range(4)]
                for c, d in enumerate(density(r, w)):
                    keep(g, c, j, row, d)

        steps(groups, starts[3], counts[3], finish)

    def fold(ref, at):
        parts = []
        for g in range(2):
            for s in range(8):
                parts.append(ref[at(g) + (pl.ds(s, 8, stride=8), slice(None))])
        while len(parts) > 1:
            parts = [parts[i] + parts[i + 1] for i in range(0, len(parts), 2)]
        return parts[0]

    def refs(grp, mid, edge):
        return mid if grp is None else edge.at[grp]

    def sem(ref, grp, *at):
        return ref.at[(0 if grp is None else 1 + grp, *at)]

    def y_scatter(grp, d):
        to = y_peer(d)
        return pltpu.make_async_remote_copy(
            refs(grp, FM, FE).at[to - base], refs(grp, RM, RE).at[d],
            sem(ys_s, grp, d), sem(ys_r, grp, d),
            device_id={"vec": to}, device_id_type=MESH,
        )

    def x_exchange(grp):
        return pltpu.make_async_remote_copy(
            refs(grp, QM, QE), refs(grp, XM, XE), sem(xs_s, grp), sem(xs_r, grp),
            device_id={"vec": partner}, device_id_type=MESH,
        )

    def y_gather(grp, d):
        here = refs(grp, out_mid, out_edge).at[y]
        return pltpu.make_async_remote_copy(
            here, here, sem(yg_s, grp, d), sem(yg_r, grp, d),
            device_id={"vec": y_peer(d)}, device_id_type=MESH,
        )

    def scatter(grp):
        for d in (2, 1, 3):
            y_scatter(grp, d).start()

    def partial_sum(grp):
        for d in range(1, NY):
            y_scatter(grp, d).wait_recv()
        got, mine = refs(grp, RM, RE), refs(grp, FM, FE)
        return (mine[y] + got[1]) + (got[2] + got[3])

    def edge_partial_sum(s, which, into):
        total = partial_sum(s)
        for d in range(NY):
            push_copy(s, which, d).wait_recv()
        extra = placed(s)
        for c in range(3):
            into[c] = total[c] + extra[c]

    def exchange(grp):
        if grp is None:
            QM[...] = partial_sum(grp)
        else:
            edge_partial_sum(grp, 0, QE.at[grp])
        x_exchange(grp).start()

    def gather(grp):
        x_exchange(grp).wait_recv()
        refs(grp, out_mid, out_edge)[y] = refs(grp, QM, QE)[...] + refs(grp, XM, XE)[...]
        for d in range(1, NY):
            y_gather(grp, d).start()

    def keep_mid(g, c, j, row, d):
        at = pl.multiple_of((row - 4) * 8, 8)
        DM[g, c, j, pl.ds(at, 8), :] = d

    def keep_edge(s):
        def keep(g, c, j, row, d):
            at = pl.multiple_of(lax.rem(row + 2 * s, 4) * 8 + 32 * (j % 2), 8)
            DE[s, g, c, j // 2, pl.ds(at, 8), :] = d

        return keep

    sweep((0, 1), (1, 2, 3, 4), (14, 12, 10, 8), keep_mid)

    @pl.loop(0, NY)
    def _(q):
        for half in range(2):
            for c in range(3):
                FM[q, half, c] = fold(DM, lambda g: (g, c, 2 * q + half))

    scatter(None)

    for s in range(2):
        spin_copy(s).wait_recv()
    for q in range(4):
        cols = slice(q * 256, (q + 1) * 256)
        got = 2.0 * permuted(SHr[:, :, cols].reshape(16, 256), by_deal)
        for s in range(2):
            for c in range(3):
                for k in range(2):
                    at = 8 * s + 2 * c + k
                    SB[(2, 20)[s] + k, c, :, cols] = jnp.broadcast_to(
                        got[at : at + 1], (8, 256)
                    )

    def push(s, g):
        far, near = 2 + 11 * s + PAD, PAD - 1 + 17 * s
        row_far, row_next = PAD - 2 + 19 * s, PAD + 3 + 9 * s
        low = PAD - 1 + 14 * s
        at0 = [pl.multiple_of((2 * c + 1 - s) * 8, 8) for c in range(3)]
        at1 = [pl.multiple_of((2 * c + s) * 8, 8) for c in range(3)]
        for j in range(BLOCKS):
            cols = (slice(None), lanes(j))
            spin = [
                (SB[(low, c) + cols] + SB[(low + 1, c) + cols])
                + (SB[(low + 2, c) + cols] + SB[(low + 3, c) + cols])
                for c in range(3)
            ]
            b2 = [R[(g, far, c) + cols] for c in range(4)]
            onsite = spin_on(b2, spin)
            u, v = [], []
            for c in range(4):
                more = R[(g, row_next, c) + cols] + 4.0 * around(R, (g, far, c), j)
                u.append(a3 * b2[c] + a4 * (more - onsite[c]))
                v.append(a4 * b2[c])
            r0 = [R[(g, near, c) + cols] for c in range(4)]
            r1 = [R[(g, row_far, c) + cols] for c in range(4)]
            for c, d in enumerate(density(r0, u)):
                E[s, g, j, pl.ds(at0[c], 8), :] = d
            for c, d in enumerate(density(r1, v)):
                E[s, g, j, pl.ds(at1[c], 8), :] = d

    def wait_halo(s, g):
        pltpu.make_async_copy(R.at[g, pl.ds(2, 2)], R.at[g, pl.ds(2, 2)], hr.at[s, g]).wait()

    chip_side = 1 - lax.rem(lat, 2)
    link_side = 1 - chip_side

    def beyond(s):
        return lax.rem(lat + LAT - 1 + 2 * s, LAT)

    def push_copy(s, which, d):
        to = y_peer(d)
        return pltpu.make_async_remote_copy(
            PBs.at[s, pl.ds(2 * (to - base), 2)], PBr.at[1 - s, d],
            ps.at[which, d], pr.at[which, d],
            device_id={"lat": beyond(s), "vec": to}, device_id_type=MESH,
        )

    def spread_sum(half, d):
        to = lax.rem(base + NY * half, VEC) + lax.rem(y + d, NY)
        return pltpu.make_async_remote_copy(
            GX.at[0, y], GX.at[half, y], bs_s.at[half, d], bs_r.at[half, d],
            device_id={"vec": to}, device_id_type=MESH,
        )

    others = [(1, 2), (1, 1), (1, 3), (0, 2), (1, 0), (0, 1), (0, 3)]

    sub = lax.broadcasted_iota(jnp.int32, (8, 128), 0)

    def placed(s):
        got = (PBr[s, 0] + PBr[s, 1]) + (PBr[s, 2] + PBr[s, 3])
        res = []
        for c in range(3):
            total = jnp.zeros((8, 128), jnp.float32)
            for half in range(2):
                here = (sub == 4 * half) | (sub == 4 * half + 1)
                moved = pltpu.roll(got[half], (4 * half - 2 * c) % 8, 0)
                total = jnp.where(here, moved, total)
            res.append(total)
        return res

    def wedge(s, groups):
        sweep(
            groups, (18 * s - 3, 16 * s - 2, 14 * s - 1, 12 * s), (4, 4, 4, 4), keep_edge(s)
        )

    def fold_push(s):
        @pl.loop(0, BLOCKS)
        def _(j):
            PBs[s, j] = fold(E, lambda g: (s, g, j))

    def fold_edge(s):
        @pl.loop(0, NY)
        def _(q):
            for c in range(3):
                FE[s, q, c] = fold(DE, lambda g: (s, g, c, q))

    s = chip_side
    for g in range(2):
        wait_halo(s, g)
    wedge(s, (0, 1))
    fold_edge(s)
    scatter(s)

    s = link_side
    wait_halo(s, 0)
    push(s, 0)
    wedge(s, (0,))
    exchange(None)
    for g in range(2):
        push(chip_side, g)
    fold_push(chip_side)
    for d in range(NY):
        push_copy(chip_side, 0, d).start()
    wait_halo(s, 1)
    push(s, 1)
    fold_push(s)
    for d in range(NY):
        push_copy(s, 1, d).start()
    wedge(s, (1,))
    fold_edge(s)
    scatter(s)
    exchange(chip_side)
    gather(None)
    edge_partial_sum(s, 1, GX.at[0, y])
    for half, d in others:
        spread_sum(half, d).start()
    gather(chip_side)

    for s in range(2):
        spin_copy(s).wait_send()
        for g in range(2):
            halo_copy(s, g).wait_send()
    for d in range(NY):
        push_copy(chip_side, 0, d).wait_send()
        push_copy(link_side, 1, d).wait_send()
    for d in range(1, NY):
        y_scatter(link_side, d).wait_send()
    for grp in (None, chip_side):
        x_exchange(grp).wait_send()
        for d in range(1, NY):
            y_scatter(grp, d).wait_send()
            y_gather(grp, d).wait()
    for half, d in others:
        spread_sum(half, d).wait()
    out_edge[link_side] = GX[0] + GX[1]


def rotate_kernel(mid_ref, edge_ref, s_ref, rot, fields):
    sub = lax.broadcasted_iota(jnp.int32, (8, 128), 0)
    top, third = sub < 4, sub < 6
    by = deal(inverse=True)
    dealt = [[] for _ in range(BLOCKS)]
    for j in range(BLOCKS):
        q, half = divmod(j, 2)
        low, high = [], []
        for c in range(3):
            mid = pltpu.roll(mid_ref[q, half, c], 4, 0)
            start, end = edge_ref[0, q, c], edge_ref[1, q, c]
            if half:
                start = pltpu.roll(start, 4, 0)
            end = jnp.where(
                third,
                pltpu.roll(end, (2 - 4 * half) % 8, 0),
                pltpu.roll(end, (6 - 4 * half) % 8, 0),
            )
            low.append(jnp.where(top, start, mid))
            high.append(jnp.where(top, mid, end))
        dealt[j] = jnp.concatenate(low + high, axis=0) * (coupling / (VECS * VEC))
    for j in range(BLOCKS):
        if j % 2 == 0:
            natural = permuted(jnp.concatenate(dealt[j : j + 2], axis=1), by)
        cols = lanes(j)
        for block in range(2):
            rows = slice(block * 8, block * 8 + 8)
            at = (j % 2) * 128
            B = [
                natural[(3 * block + c) * 8 : (3 * block + c + 1) * 8, at : at + 128]
                for c in range(3)
            ]
            S = [s_ref[c, rows, cols] for c in range(3)]
            square = B[0] * B[0] + B[1] * B[1] + B[2] * B[2]
            size = jnp.sqrt(square)
            half_angle = 0.5 * size
            sin_h, cos_h = jnp.sin(half_angle), jnp.cos(half_angle)
            some = size > 0.0
            safe = jnp.where(some, size, 1.0)
            ratio = jnp.where(some, sin_h / safe, 0.5)
            cosine = 1.0 - 2.0 * (sin_h * sin_h)
            sine_ratio = 2.0 * (ratio * cos_h)
            along = 2.0 * (ratio * ratio) * (B[0] * S[0] + B[1] * S[1] + B[2] * S[2])
            cross = (
                B[1] * S[2] - B[2] * S[1],
                B[2] * S[0] - B[0] * S[2],
                B[0] * S[1] - B[1] * S[0],
            )
            for c in range(3):
                fields[c, rows, cols] = B[c]
                rot[c, rows, cols] = (cosine * S[c] + sine_ratio * cross[c]) + along * B[c]


def shards(vectors, classical_spins, coefficients):
    f32 = jnp.float32
    vmem = pl.BlockSpec(memory_space=pltpu.VMEM)
    dma = pltpu.SemaphoreType.DMA
    mid, edge = (NY, 2, 3, 8, 128), (2, NY, 3, 8, 128)
    parts = pl.pallas_call(
        field_kernel,
        name="fields",
        out_shape=(jax.ShapeDtypeStruct(mid, f32), jax.ShapeDtypeStruct(edge, f32)),
        in_specs=[
            pl.BlockSpec(memory_space=pltpu.SMEM),
            pl.BlockSpec(memory_space=pl.ANY),
            pl.BlockSpec(memory_space=pl.ANY),
        ],
        out_specs=(vmem, vmem),
        scratch_shapes=[
            pltpu.VMEM((4, VECS, ROWS, COLS), jnp.bfloat16),
            pltpu.VMEM((3, ROWS, COLS), f32),
            *[pltpu.VMEM((2, 24, 4, 8, COLS), f32)] * 4,
            pltpu.VMEM((24, 3, 8, COLS), f32),
            pltpu.VMEM((2, 8, COLS), f32),
            pltpu.VMEM((2, 8, COLS), f32),
            pltpu.VMEM((2, 3, BLOCKS, 64, 128), f32),
            pltpu.VMEM((2, 2, 3, NY, 64, 128), f32),
            pltpu.VMEM((2, 2, BLOCKS, 64, 128), f32),
            pltpu.VMEM((2, BLOCKS, 8, 128), f32),
            pltpu.VMEM((2, NY, 2, 8, 128), f32),
            pltpu.VMEM(mid, f32), pltpu.VMEM(mid, f32),
            pltpu.VMEM(mid[1:], f32), pltpu.VMEM(mid[1:], f32),
            pltpu.VMEM(edge, f32), pltpu.VMEM(edge, f32),
            pltpu.VMEM((2, 3, 8, 128), f32), pltpu.VMEM((2, 3, 8, 128), f32),
            pltpu.VMEM((3 * ROWS, COLS), f32),
            pltpu.VMEM(edge, f32),
            dma((2,)), dma, dma((2, 2)), dma((2, 2)), dma((2,)), dma((2,)),
            dma((2, NY)), dma((2, NY)),
            dma((3, NY)), dma((3, NY)), dma((3,)), dma((3,)), dma((3, NY)), dma((3, NY)),
            dma((2, NY)), dma((2, NY)),
        ],
        compiler_params=pltpu.CompilerParams(
            collective_id=0, has_side_effects=True, vmem_limit_bytes=60 << 20
        ),
    )(coefficients, vectors, classical_spins)
    out = jax.ShapeDtypeStruct((3, ROWS, COLS), f32)
    rotated, fields = pl.pallas_call(
        rotate_kernel,
        name="rotate",
        out_shape=(out, out),
        in_specs=[vmem, vmem, vmem],
        out_specs=(vmem, vmem),
    )(*parts, classical_spins)
    return rotated, fields


def solution(mesh):
    placed = (P(None, "vec", "lat", None), P(None, "lat", None), P())
    return jax.shard_map(
        shards,
        mesh=mesh,
        in_specs=placed,
        out_specs=(P(None, "lat", None), P(None, "lat", None)),
        check_vma=False,
    )
```

```python
import functools

import jax
import jax.numpy as jnp
from jax import lax
from jax.experimental import pallas as pl
from jax.experimental.pallas import tpu as pltpu
from jax.sharding import PartitionSpec as P

MESH = pl.DeviceIdType.MESH
LAT, VEC, NY = 16, 8, 4
ROWS, COLS, VECS = 16, 1024, 16
BLOCKS = COLS // 128
PAD = 4
STEPS_EACH = 4
coupling = 2.0
inverse_bound = 1.0 / 6.5


def spin_on(state, spin):
    x, y, z = spin
    p0, p1, p2, p3 = state
    return (
        (z * p0 + x * p2) + y * p3,
        (z * p1 + x * p3) - y * p2,
        (x * p0 - y * p1) - z * p2,
        (x * p1 + y * p0) - z * p3,
    )


def density(r, w):
    return (
        (r[0] * w[2] + r[1] * w[3]) + (r[2] * w[0] + r[3] * w[1]),
        (r[0] * w[3] - r[1] * w[2]) - (r[2] * w[1] - r[3] * w[0]),
        (r[0] * w[0] + r[1] * w[1]) - (r[2] * w[2] + r[3] * w[3]),
    )


def bf16_parts(x):
    high = x.astype(jnp.bfloat16)
    rest = x - high.astype(jnp.float32)
    mid = rest.astype(jnp.bfloat16)
    low = (rest - mid.astype(jnp.float32)).astype(jnp.bfloat16)
    return jnp.concatenate([high, mid, low], axis=0)


def permuted(x, by):
    n = x.shape[0]
    got = jnp.dot(bf16_parts(x), by, preferred_element_type=jnp.float32)
    return (got[:n] + got[n : 2 * n]) + got[2 * n :]


def deal(inverse=False):
    here = lax.broadcasted_iota(jnp.int32, (256, 256), int(inverse))
    there = lax.broadcasted_iota(jnp.int32, (256, 256), int(not inverse))
    source = jnp.where(there < 128, 2 * there, 2 * there - 255)
    return jnp.where(here == source, 1.0, 0.0).astype(jnp.bfloat16)


def lanes(j):
    j = j % BLOCKS
    return slice(j * 128, (j + 1) * 128)


def field_kernel(
    coef, x_hbm, s_hbm, out_mid, out_edge,
    xv, s_vmem, R, W3, W2, W1, SB, SHs, SHr, DM, DE, E, PBs, PBr,
    FM, RM, QM, XM, FE, RE, QE, XE, SP, GX,
    xsem, ssem, hs, hr, ss, sr, ps, pr, ys_s, ys_r, xs_s, xs_r, yg_s, yg_r, bs_s, bs_r,
):
    lat, vec = lax.axis_index("lat"), lax.axis_index("vec")
    prev, nxt = lax.rem(lat + LAT - 1, LAT), lax.rem(lat + 1, LAT)
    y = lax.rem(vec, NY)
    base = vec - y
    partner = lax.rem(vec + NY, VEC)

    def y_peer(d):
        return base + lax.rem(y + d, NY)

    load_spins = pltpu.make_async_copy(s_hbm, s_vmem, ssem)
    load_spins.start()
    def load(g):
        half = (slice(None), pl.ds(8 * g, 8))
        return pltpu.make_async_copy(x_hbm.at[half], xv.at[half], xsem.at[g])

    load(0).start()
    load(1).start()

    barrier = pltpu.get_barrier_semaphore()
    for to in (prev, nxt):
        pl.semaphore_signal(barrier, 1, device_id={"lat": to}, device_id_type=MESH)
    for to in (y_peer(1), y_peer(2), y_peer(3), partner):
        pl.semaphore_signal(barrier, 1, device_id={"vec": to}, device_id_type=MESH)

    c0, c1, c2, c3, c4 = (coef[k] for k in range(5))
    h = inverse_bound
    a0 = c0 - c2 + c4
    a1 = (3.0 * c3 - c1) * h
    a2 = (2.0 * c2 - 8.0 * c4) * (h * h)
    a3 = c3 * (-4.0 * h * h * h)
    a4 = c4 * (8.0 * h * h * h * h)

    by_deal = deal()

    def swap(order):
        n = 16 * len(order)
        m = lax.broadcasted_iota(jnp.int32, (n, 256), 0)
        k = lax.broadcasted_iota(jnp.int32, (n, 256), 1)
        at = m // 16
        row = jnp.where(at < 2, at, at + 12) if order[0] == 0 else at + 2
        return jnp.where((k % 16 == row) & (k // 16 == m % 16), 1.0, 0.0).astype(jnp.bfloat16)

    def swap_ends():
        m = lax.broadcasted_iota(jnp.int32, (32, 128), 0)
        k = lax.broadcasted_iota(jnp.int32, (32, 128), 1)
        at = m // 8
        row = jnp.where(at < 2, at, at + 12)
        return jnp.where((k % 16 == row) & (k // 16 == m % 8), 1.0, 0.0).astype(jnp.bfloat16)

    def spread_ends(g, by):
        for c in range(4):
            for q in range(4):
                cols = slice(q * 256, (q + 1) * 256)
                got = jnp.dot(
                    by,
                    xv[c, 8 * g : 8 * g + 8, :, cols].reshape(128, 256),
                    preferred_element_type=jnp.float32,
                ).astype(jnp.bfloat16)
                got = jnp.dot(got, by_deal, preferred_element_type=jnp.float32)
                for at, row in enumerate((0, 1, 14, 15)):
                    R[g, PAD + row, c, :, cols] = got[8 * at : 8 * at + 8]

    def spread(order):
        by = swap(order)

        @pl.loop(0, 4)
        def _(c):
            for q in range(4):
                cols = slice(q * 256, (q + 1) * 256)
                got = jnp.dot(
                    by, xv[c, :, :, cols].reshape(256, 256), preferred_element_type=jnp.float32
                ).astype(jnp.bfloat16)
                got = jnp.dot(got, by_deal, preferred_element_type=jnp.float32)
                for at, row in enumerate(order):
                    for g in range(2):
                        lo = at * 16 + g * 8
                        R[g, PAD + row, c, :, cols] = got[lo : lo + 8]

    def spin_copy(s):
        return pltpu.make_async_remote_copy(
            SHs.at[s], SHr.at[1 - s], ss.at[s], sr.at[1 - s],
            device_id={"lat": (prev, nxt)[s]}, device_id_type=MESH,
        )

    def halo_copy(s, g):
        src, dst = 4 + 14 * s, 20 - 18 * s
        return pltpu.make_async_remote_copy(
            R.at[g, pl.ds(src, 2)], R.at[g, pl.ds(dst, 2)], hs.at[s, g], hr.at[1 - s, g],
            device_id={"lat": lax.rem(lat + LAT - 1 + 2 * s, LAT)}, device_id_type=MESH,
        )

    load_spins.wait()
    for c in range(3):
        for k in range(2):
            q = 2 * c + k
            SHs[0, q : q + 1, :] = s_vmem[c, k : k + 1, :]
            SHs[1, q : q + 1, :] = s_vmem[c, 14 + k : 15 + k, :]
    for s in range(2):
        SHs[s, 6:8, :] = jnp.zeros((2, COLS), jnp.float32)
    by_ends = swap_ends()
    for g in range(2):
        load(g).wait()
        spread_ends(g, by_ends)
        if g == 0:
            pl.semaphore_wait(barrier, 2 + 4)
            for s in range(2):
                spin_copy(s).start()
        for s in (lax.rem(lat, 2), 1 - lax.rem(lat, 2)):
            halo_copy(s, g).start()

    for q in range(4):
        cols = slice(q * 256, (q + 1) * 256)
        SP[:, cols] = permuted(s_vmem[:, :, cols].reshape(3 * ROWS, 256), by_deal)
    zero = jnp.zeros((8, COLS), jnp.float32)
    for row in range(ROWS):
        for c in range(3):
            at = c * ROWS + row
            SB[PAD + row, c] = jnp.broadcast_to(2.0 * SP[at : at + 1, :], (8, COLS))

    spread(tuple(range(2, 14)))
    for c in range(3):
        for row in (1, 22):
            SB[row, c] = zero
    for g in range(2):
        for row in (0, 1, 22, 23):
            for c in range(4):
                R[g, row, c] = zero
        for s in range(2):
            for j in range(BLOCKS):
                E[s, g, j, 48:64, :] = jnp.zeros((16, 128), jnp.float32)

    lane = lax.broadcasted_iota(jnp.int32, (8, 128), 1)
    first, last = lane == 0, lane == 127

    def around(ref, at, j):
        other = ref[at + (slice(None), lanes(j ^ 1))]
        if j % 2 == 0:
            return other + pltpu.roll(
                jnp.where(last, ref[at + (slice(None), lanes(j - 1))], other), 1, 1
            )
        return other + pltpu.roll(
            jnp.where(first, ref[at + (slice(None), lanes(j + 1))], other), 127, 1
        )

    def hop(src, g, row, j):
        cols = (slice(None), lanes(j))
        spin = [SB[(PAD + row, c) + cols] for c in range(3)]
        state = [src[(g, PAD + row, c) + cols] for c in range(4)]
        onsite = spin_on(state, spin)
        res = []
        for c in range(4):
            n = src[(g, PAD + row - 1, c) + cols] + src[(g, PAD + row + 1, c) + cols]
            res.append((n + around(src, (g, PAD + row, c), j)) - onsite[c])
        return res

    def steps(groups, start, count, body):
        each = 2

        @pl.loop(0, count // each)
        def _(i):
            for k in range(each):
                for g in groups:
                    body(g, start + each * i + k)

    def sweep(groups, starts, counts, keep):
        def third(g, row):
            for j in range(BLOCKS):
                cols = (slice(None), lanes(j))
                got = hop(R, g, row, j)
                for c in range(4):
                    W3[(g, PAD + row, c) + cols] = a4 * got[c] + a3 * R[(g, PAD + row, c) + cols]

        steps(groups, starts[0], counts[0], third)

        for level, (src, dst, a) in enumerate(((W3, W2, a2), (W2, W1, a1)), 1):
            def lower(g, row):
                for j in range(BLOCKS):
                    cols = (slice(None), lanes(j))
                    got = hop(src, g, row, j)
                    for c in range(4):
                        dst[(g, PAD + row, c) + cols] = got[c] + a * R[(g, PAD + row, c) + cols]

            steps(groups, starts[level], counts[level], lower)

        def finish(g, row):
            for j in range(BLOCKS):
                cols = (slice(None), lanes(j))
                got = hop(W1, g, row, j)
                r = [R[(g, PAD + row, c) + cols] for c in range(4)]
                w = [got[c] + a0 * r[c] for c in range(4)]
                for c, d in enumerate(density(r, w)):
                    keep(g, c, j, row, d)

        steps(groups, starts[3], counts[3], finish)

    def fold(ref, at):
        parts = []
        for g in range(2):
            for s in range(8):
                parts.append(ref[at(g) + (pl.ds(s, 8, stride=8), slice(None))])
        while len(parts) > 1:
            parts = [parts[i] + parts[i + 1] for i in range(0, len(parts), 2)]
        return parts[0]

    def refs(grp, mid, edge):
        return mid if grp is None else edge.at[grp]

    def sem(ref, grp, *at):
        return ref.at[(0 if grp is None else 1 + grp, *at)]

    def y_scatter(grp, d):
        to = y_peer(d)
        return pltpu.make_async_remote_copy(
            refs(grp, FM, FE).at[to - base], refs(grp, RM, RE).at[d],
            sem(ys_s, grp, d), sem(ys_r, grp, d),
            device_id={"vec": to}, device_id_type=MESH,
        )

    def x_exchange(grp):
        return pltpu.make_async_remote_copy(
            refs(grp, QM, QE), refs(grp, XM, XE), sem(xs_s, grp), sem(xs_r, grp),
            device_id={"vec": partner}, device_id_type=MESH,
        )

    def y_gather(grp, d):
        here = refs(grp, out_mid, out_edge).at[y]
        return pltpu.make_async_remote_copy(
            here, here, sem(yg_s, grp, d), sem(yg_r, grp, d),
            device_id={"vec": y_peer(d)}, device_id_type=MESH,
        )

    def scatter(grp):
        for d in (2, 1, 3):
            y_scatter(grp, d).start()

    def partial_sum(grp):
        for d in range(1, NY):
            y_scatter(grp, d).wait_recv()
        got, mine = refs(grp, RM, RE), refs(grp, FM, FE)
        return (mine[y] + got[1]) + (got[2] + got[3])

    def edge_partial_sum(s, which, into):
        total = partial_sum(s)
        for d in range(NY):
            push_copy(s, which, d).wait_recv()
        extra = placed(s)
        for c in range(3):
            into[c] = total[c] + extra[c]

    def exchange(grp):
        edge_partial_sum(grp, 0, QE.at[grp])
        x_exchange(grp).start()

    def gather(grp):
        x_exchange(grp).wait_recv()
        refs(grp, out_mid, out_edge)[y] = refs(grp, QM, QE)[...] + refs(grp, XM, XE)[...]
        for d in range(1, NY):
            y_gather(grp, d).start()

    def keep_mid(g, c, j, row, d):
        at = pl.multiple_of((row - 4) * 8, 8)
        DM[g, c, j, pl.ds(at, 8), :] = d

    def keep_edge(s):
        def keep(g, c, j, row, d):
            at = pl.multiple_of(lax.rem(row + 2 * s, 4) * 8 + 32 * (j % 2), 8)
            DE[s, g, c, j // 2, pl.ds(at, 8), :] = d

        return keep

    sweep((0, 1), (1, 2, 3, 4), (14, 12, 10, 8), keep_mid)

    @pl.loop(0, NY)
    def _(q):
        for half in range(2):
            for c in range(3):
                FM[q, half, c] = fold(DM, lambda g: (g, c, 2 * q + half))

    scatter(None)

    for s in range(2):
        spin_copy(s).wait_recv()
    for q in range(4):
        cols = slice(q * 256, (q + 1) * 256)
        got = 2.0 * permuted(SHr[:, :, cols].reshape(16, 256), by_deal)
        for s in range(2):
            for c in range(3):
                for k in range(2):
                    at = 8 * s + 2 * c + k
                    SB[(2, 20)[s] + k, c, :, cols] = jnp.broadcast_to(
                        got[at : at + 1], (8, 256)
                    )

    def push(s, g):
        far, near = 2 + 11 * s + PAD, PAD - 1 + 17 * s
        row_far, row_next = PAD - 2 + 19 * s, PAD + 3 + 9 * s
        low = PAD - 1 + 14 * s
        at0 = [pl.multiple_of((2 * c + 1 - s) * 8, 8) for c in range(3)]
        at1 = [pl.multiple_of((2 * c + s) * 8, 8) for c in range(3)]
        for j in range(BLOCKS):
            cols = (slice(None), lanes(j))
            spin = [
                (SB[(low, c) + cols] + SB[(low + 1, c) + cols])
                + (SB[(low + 2, c) + cols] + SB[(low + 3, c) + cols])
                for c in range(3)
            ]
            b2 = [R[(g, far, c) + cols] for c in range(4)]
            onsite = spin_on(b2, spin)
            u, v = [], []
            for c in range(4):
                more = R[(g, row_next, c) + cols] + 4.0 * around(R, (g, far, c), j)
                u.append(a3 * b2[c] + a4 * (more - onsite[c]))
                v.append(a4 * b2[c])
            r0 = [R[(g, near, c) + cols] for c in range(4)]
            r1 = [R[(g, row_far, c) + cols] for c in range(4)]
            for c, d in enumerate(density(r0, u)):
                E[s, g, j, pl.ds(at0[c], 8), :] = d
            for c, d in enumerate(density(r1, v)):
                E[s, g, j, pl.ds(at1[c], 8), :] = d

    def wait_halo(s, g):
        pltpu.make_async_copy(R.at[g, pl.ds(2, 2)], R.at[g, pl.ds(2, 2)], hr.at[s, g]).wait()

    chip_side = 1 - lax.rem(lat, 2)
    link_side = 1 - chip_side

    def beyond(s):
        return lax.rem(lat + LAT - 1 + 2 * s, LAT)

    def push_copy(s, which, d):
        to = y_peer(d)
        return pltpu.make_async_remote_copy(
            PBs.at[s, pl.ds(2 * (to - base), 2)], PBr.at[1 - s, d],
            ps.at[which, d], pr.at[which, d],
            device_id={"lat": beyond(s), "vec": to}, device_id_type=MESH,
        )

    def spread_sum(half, d):
        to = lax.rem(base + NY * half, VEC) + lax.rem(y + d, NY)
        return pltpu.make_async_remote_copy(
            GX.at[0, y], GX.at[half, y], bs_s.at[half, d], bs_r.at[half, d],
            device_id={"vec": to}, device_id_type=MESH,
        )

    others = [(1, 2), (1, 1), (1, 3), (0, 2), (1, 0), (0, 1), (0, 3)]

    sub = lax.broadcasted_iota(jnp.int32, (8, 128), 0)

    def placed(s):
        got = (PBr[s, 0] + PBr[s, 1]) + (PBr[s, 2] + PBr[s, 3])
        res = []
        for c in range(3):
            total = jnp.zeros((8, 128), jnp.float32)
            for half in range(2):
                here = (sub == 4 * half) | (sub == 4 * half + 1)
                moved = pltpu.roll(got[half], (4 * half - 2 * c) % 8, 0)
                total = jnp.where(here, moved, total)
            res.append(total)
        return res

    def wedge(s, groups):
        sweep(
            groups, (18 * s - 3, 16 * s - 2, 14 * s - 1, 12 * s), (4, 4, 4, 4), keep_edge(s)
        )

    def fold_push(s):
        @pl.loop(0, BLOCKS)
        def _(j):
            PBs[s, j] = fold(E, lambda g: (s, g, j))

    def fold_edge(s):
        @pl.loop(0, NY)
        def _(q):
            for c in range(3):
                FE[s, q, c] = fold(DE, lambda g: (s, g, c, q))

    s = chip_side
    for g in range(2):
        wait_halo(s, g)
    wedge(s, (0, 1))
    fold_edge(s)
    scatter(s)

    s = link_side
    wait_halo(s, 0)
    push(s, 0)
    wedge(s, (0,))
    QM[...] = partial_sum(None)
    for g in range(2):
        push(chip_side, g)
    fold_push(chip_side)
    for d in range(NY):
        push_copy(chip_side, 0, d).start()
    wait_halo(s, 1)
    push(s, 1)
    fold_push(s)
    for d in range(NY):
        push_copy(s, 1, d).start()
    x_exchange(None).start()
    wedge(s, (1,))
    fold_edge(s)
    scatter(s)
    exchange(chip_side)
    gather(None)
    edge_partial_sum(s, 1, GX.at[0, y])
    for half, d in others:
        spread_sum(half, d).start()
    gather(chip_side)

    for s in range(2):
        spin_copy(s).wait_send()
        for g in range(2):
            halo_copy(s, g).wait_send()
    for d in range(NY):
        push_copy(chip_side, 0, d).wait_send()
        push_copy(link_side, 1, d).wait_send()
    for d in range(1, NY):
        y_scatter(link_side, d).wait_send()
    for grp in (None, chip_side):
        x_exchange(grp).wait_send()
        for d in range(1, NY):
            y_scatter(grp, d).wait_send()
            y_gather(grp, d).wait()
    for half, d in others:
        spread_sum(half, d).wait()
    out_edge[link_side] = GX[0] + GX[1]


def rotate_kernel(mid_ref, edge_ref, s_ref, rot, fields):
    sub = lax.broadcasted_iota(jnp.int32, (8, 128), 0)
    top, third = sub < 4, sub < 6
    by = deal(inverse=True)
    dealt = [[] for _ in range(BLOCKS)]
    for j in range(BLOCKS):
        q, half = divmod(j, 2)
        low, high = [], []
        for c in range(3):
            mid = pltpu.roll(mid_ref[q, half, c], 4, 0)
            start, end = edge_ref[0, q, c], edge_ref[1, q, c]
            if half:
                start = pltpu.roll(start, 4, 0)
            end = jnp.where(
                third,
                pltpu.roll(end, (2 - 4 * half) % 8, 0),
                pltpu.roll(end, (6 - 4 * half) % 8, 0),
            )
            low.append(jnp.where(top, start, mid))
            high.append(jnp.where(top, mid, end))
        dealt[j] = jnp.concatenate(low + high, axis=0) * (coupling / (VECS * VEC))
    for j in range(BLOCKS):
        if j % 2 == 0:
            natural = permuted(jnp.concatenate(dealt[j : j + 2], axis=1), by)
        cols = lanes(j)
        for block in range(2):
            rows = slice(block * 8, block * 8 + 8)
            at = (j % 2) * 128
            B = [
                natural[(3 * block + c) * 8 : (3 * block + c + 1) * 8, at : at + 128]
                for c in range(3)
            ]
            S = [s_ref[c, rows, cols] for c in range(3)]
            square = B[0] * B[0] + B[1] * B[1] + B[2] * B[2]
            size = jnp.sqrt(square)
            half_angle = 0.5 * size
            sin_h, cos_h = jnp.sin(half_angle), jnp.cos(half_angle)
            some = size > 0.0
            safe = jnp.where(some, size, 1.0)
            ratio = jnp.where(some, sin_h / safe, 0.5)
            cosine = 1.0 - 2.0 * (sin_h * sin_h)
            sine_ratio = 2.0 * (ratio * cos_h)
            along = 2.0 * (ratio * ratio) * (B[0] * S[0] + B[1] * S[1] + B[2] * S[2])
            cross = (
                B[1] * S[2] - B[2] * S[1],
                B[2] * S[0] - B[0] * S[2],
                B[0] * S[1] - B[1] * S[0],
            )
            for c in range(3):
                fields[c, rows, cols] = B[c]
                rot[c, rows, cols] = (cosine * S[c] + sine_ratio * cross[c]) + along * B[c]


def shards(vectors, classical_spins, coefficients):
    f32 = jnp.float32
    vmem = pl.BlockSpec(memory_space=pltpu.VMEM)
    dma = pltpu.SemaphoreType.DMA
    mid, edge = (NY, 2, 3, 8, 128), (2, NY, 3, 8, 128)
    parts = pl.pallas_call(
        field_kernel,
        name="fields",
        out_shape=(jax.ShapeDtypeStruct(mid, f32), jax.ShapeDtypeStruct(edge, f32)),
        in_specs=[
            pl.BlockSpec(memory_space=pltpu.SMEM),
            pl.BlockSpec(memory_space=pl.ANY),
            pl.BlockSpec(memory_space=pl.ANY),
        ],
        out_specs=(vmem, vmem),
        scratch_shapes=[
            pltpu.VMEM((4, VECS, ROWS, COLS), jnp.bfloat16),
            pltpu.VMEM((3, ROWS, COLS), f32),
            *[pltpu.VMEM((2, 24, 4, 8, COLS), f32)] * 4,
            pltpu.VMEM((24, 3, 8, COLS), f32),
            pltpu.VMEM((2, 8, COLS), f32),
            pltpu.VMEM((2, 8, COLS), f32),
            pltpu.VMEM((2, 3, BLOCKS, 64, 128), f32),
            pltpu.VMEM((2, 2, 3, NY, 64, 128), f32),
            pltpu.VMEM((2, 2, BLOCKS, 64, 128), f32),
            pltpu.VMEM((2, BLOCKS, 8, 128), f32),
            pltpu.VMEM((2, NY, 2, 8, 128), f32),
            pltpu.VMEM(mid, f32), pltpu.VMEM(mid, f32),
            pltpu.VMEM(mid[1:], f32), pltpu.VMEM(mid[1:], f32),
            pltpu.VMEM(edge, f32), pltpu.VMEM(edge, f32),
            pltpu.VMEM((2, 3, 8, 128), f32), pltpu.VMEM((2, 3, 8, 128), f32),
            pltpu.VMEM((3 * ROWS, COLS), f32),
            pltpu.VMEM(edge, f32),
            dma((2,)), dma, dma((2, 2)), dma((2, 2)), dma((2,)), dma((2,)),
            dma((2, NY)), dma((2, NY)),
            dma((3, NY)), dma((3, NY)), dma((3,)), dma((3,)), dma((3, NY)), dma((3, NY)),
            dma((2, NY)), dma((2, NY)),
        ],
        compiler_params=pltpu.CompilerParams(
            collective_id=0, has_side_effects=True, vmem_limit_bytes=60 << 20
        ),
    )(coefficients, vectors, classical_spins)
    out = jax.ShapeDtypeStruct((3, ROWS, COLS), f32)
    rotated, fields = pl.pallas_call(
        rotate_kernel,
        name="rotate",
        out_shape=(out, out),
        in_specs=[vmem, vmem, vmem],
        out_specs=(vmem, vmem),
    )(*parts, classical_spins)
    return rotated, fields


def solution(mesh):
    placed = (P(None, "vec", "lat", None), P(None, "lat", None), P())
    return jax.shard_map(
        shards,
        mesh=mesh,
        in_specs=placed,
        out_specs=(P(None, "lat", None), P(None, "lat", None)),
        check_vma=False,
    )
```
